32 devices in a mesh: seq: 8 (over z, x), tensor: 4 (over y, core).
Axes of the slice: x: 2, y: 2, z: 4, core: 2. Of those that a mesh axis runs over, the one named last changes fastest.
Arguments:
- patches: bfloat16 [4096, 640], P('seq'), may hold values from -6 to 6
- keep_lists: int32 [16, 128], P('seq'), may hold values from 0 to 255, as said below
- visible_counts: int32 [16], P('seq'), may hold values from 76 to 128
- embed_weight: bfloat16 [640, 2560], replicated, may hold values from -0.25 to 0.25
- position_table: bfloat16 [256, 2560], replicated, may hold values from -6 to 6
- local_gain: float32 [2560], replicated, may hold values from 0.5 to 1.5
- local_projection: bfloat16 [2560, 16, 384], P('seq', 'tensor'), as said below
- local_output: bfloat16 [2560, 2048], P('seq', 'tensor'), may hold values from -0.125 to 0.125
- global_gain: float32 [2560], replicated, may hold values from 0.5 to 1.5
- global_projection: bfloat16 [2560, 16, 384], P('seq', 'tensor'), as said below
- global_output: bfloat16 [2560, 2048], P('seq', 'tensor'), may hold values from -0.125 to 0.125
Outputs:
- encoded: bfloat16 [16, 256, 2560], P(None, 'seq', 'tensor')
The draws below stay inside these ranges and needn't reach their ends.
Inputs may be any that keep to these rules, and one draw needn't show every extreme that they name: `keep_lists`: each row holds 128 different positions within a window; its first visible_counts entries are the window's visible patches, the others masked ones. `local_projection`: entries lie within plus or minus 16 times 2560 ** -0.5. `global_projection`: entries lie within plus or minus 16 times 2560 ** -0.5.
All inputs are finite; a program needn't handle non-finite values.
Results may differ from the reference program's by a relative error of at most 0.008.
Values may be sent and summed in bfloat16 or wider, within the bound.
No kernel may reach another device: no remote copies, remote signals or barrier semaphores. Data moves between devices by JAX's collectives and lax.ppermute only.
A program may use at most 128 MiB of HBM per device.

```python
import jax
import jax.numpy as jnp
from jax import lax

D = 2560
HEAD = 128
HEADS = 16
PATCH_IN = 640
WIN_TOK = 256
KEEP = 128
WINDOWS = 16
TOKENS = 4096


def projection_draw(key):
    normal_part = jnp.clip(jax.random.normal(key, (D, HEADS, 3 * HEAD), jnp.float32), -4.0, 4.0) * D ** (-0.5)
    return normal_part.astype(jnp.bfloat16)


def draw_local_projection(key, part):
    return projection_draw(jax.random.fold_in(key, 11))


def draw_global_projection(key, part):
    return projection_draw(jax.random.fold_in(key, 23))


def one_window(window_key):
    return jax.random.permutation(window_key, WIN_TOK)[:KEEP]


def draw_keep_lists(key, part):
    window_keys = jax.random.split(jax.random.fold_in(key, 5), WINDOWS)
    return jax.vmap(one_window)(window_keys).astype(jnp.int32)


def draw_visible_counts(key, part):
    lowest = KEEP * 3 // 5
    drawn = jax.random.randint(jax.random.fold_in(key, 1), (WINDOWS,), lowest, KEEP + 1)
    chosen = jax.random.randint(jax.random.fold_in(key, 2), (), 0, WINDOWS)
    return jnp.where(jnp.arange(WINDOWS) == chosen, KEEP, drawn).astype(jnp.int32)


def levels(key, dims, cuts, low, high):
    def one(position, blocks):
        heights = jax.random.uniform(jax.random.fold_in(jax.random.fold_in(key, 6), position), (blocks,), jnp.float32, low / len(cuts), high / len(cuts))
        return jnp.repeat(jnp.exp(heights), dims[position] // blocks).reshape((-1,) + (1,) * (len(dims) - position - 1))

    factor_of = one(*cuts[0])
    for cut in cuts[1:]:
        factor_of = factor_of * one(*cut)
    return factor_of


def gaussian(rng, shape, scale, most, cuts=(), kind=jnp.bfloat16):
    entries = scale * jax.random.normal(rng, shape, jnp.float32)
    if cuts:
        entries = entries * levels(rng, shape, cuts, -0.22, 0.18)
    return jnp.clip(entries, -most, most).astype(kind)


def setup_inputs(seed: int = 0) -> dict:
    keys = jax.random.split(jax.random.key(seed), 12)
    return {
        "patches": gaussian(keys[0], (TOKENS, PATCH_IN), 1.0, 6.0, ((0, 8),)),
        "keep_lists": draw_keep_lists(jax.random.fold_in(keys[11], 71), 0),
        "visible_counts": draw_visible_counts(jax.random.fold_in(keys[11], 71), 0),
        "embed_weight": gaussian(keys[3], (PATCH_IN, D), PATCH_IN ** -0.5, 0.25),
        "position_table": gaussian(keys[4], (WIN_TOK, D), 1.0, 6.0),
        "local_gain": jnp.clip(1.0 + 0.1 * jax.random.normal(keys[5], (D,), jnp.float32), 0.5, 1.5),
        "local_projection": draw_local_projection(jax.random.fold_in(keys[11], 71), 0),
        "local_output": gaussian(keys[7], (D, HEADS * HEAD), (HEADS * HEAD) ** -0.5, 0.125, ((0, 8), (1, 4))),
        "global_gain": jnp.clip(1.0 + 0.1 * jax.random.normal(keys[8], (D,), jnp.float32), 0.5, 1.5),
        "global_projection": draw_global_projection(jax.random.fold_in(keys[11], 71), 0),
        "global_output": gaussian(keys[10], (D, HEADS * HEAD), (HEADS * HEAD) ** -0.5, 0.125, ((0, 8), (1, 4))),
    }


EPSILON = 1e-05

def normed(values, gain):
    floats = values.astype(jnp.float32)
    center = floats - lax.optimization_barrier(jnp.mean(floats, axis=-1, keepdims=True))
    spread = lax.optimization_barrier(jnp.mean(center * center, axis=-1, keepdims=True))
    return (center * lax.rsqrt(spread + EPSILON) * gain).astype(jnp.bfloat16)

def attend(heads, allowed, width):
    queries = heads[..., :width].astype(jnp.float32)
    key_part = heads[..., width:2 * width].astype(jnp.float32)
    value_part = heads[..., 2 * width:].astype(jnp.float32)
    scores = jnp.einsum('gqhe,gkhe->ghqk', queries, key_part) * width ** (-0.5)
    scores = jnp.where(allowed[:, None], scores, -jnp.inf)
    top = lax.optimization_barrier(jnp.max(scores, axis=-1, keepdims=True))
    weights = jnp.exp(scores - top)
    weights = (weights / lax.optimization_barrier(jnp.sum(weights, axis=-1, keepdims=True))).astype(jnp.bfloat16)
    return jnp.einsum('ghqk,gkhe->gqhe', weights.astype(jnp.float32), value_part).astype(jnp.bfloat16)

def reference(patches, keep_lists, visible_counts, embed_weight, position_table, local_gain, local_projection, local_output, global_gain, global_projection, global_output):
    windows, slots = keep_lists.shape
    tiles = patches.reshape(windows, WIN_TOK, PATCH_IN)
    picked = jnp.take_along_axis(tiles, keep_lists[:, :, None], axis=1)
    embedded = jnp.einsum('wkp,pd->wkd', picked.astype(jnp.float32), embed_weight.astype(jnp.float32))
    embedded = embedded + position_table[keep_lists].astype(jnp.float32)
    start = embedded.astype(jnp.bfloat16)
    visible = jnp.arange(slots, dtype=jnp.int32)[None, :] < visible_counts[:, None]
    allowed = visible[:, None, :] | jnp.eye(slots, dtype=bool)[None]
    local_heads = jnp.einsum('wkd,dhe->wkhe', normed(start, local_gain).astype(jnp.float32), local_projection.astype(jnp.float32)).astype(jnp.bfloat16)
    local_mixed = attend(local_heads, allowed, HEAD)
    local_table = local_output.reshape(D, HEADS, HEAD).astype(jnp.float32)
    after_local = (start.astype(jnp.float32) + jnp.einsum('wkhe,dhe->wkd', local_mixed.astype(jnp.float32), local_table)).astype(jnp.bfloat16)
    window_ids = jnp.arange(windows, dtype=jnp.int32)[:, None]
    regrouped = jnp.zeros((windows, WIN_TOK, D), jnp.bfloat16).at[window_ids, keep_lists].set(after_local)
    present = jnp.zeros((windows, WIN_TOK), dtype=bool).at[window_ids, keep_lists].set(visible)
    by_position = jnp.transpose(regrouped, (1, 0, 2))
    present_by_position = jnp.transpose(present)
    eye_windows = jnp.eye(windows, dtype=bool)
    global_table = global_output.reshape(D, HEADS, HEAD).astype(jnp.float32)
    global_weights = global_projection.astype(jnp.float32)

    def one_position(packed):
        rows, marks = packed
        heads = jnp.einsum('wd,dhe->whe', normed(rows, global_gain).astype(jnp.float32), global_weights).astype(jnp.bfloat16)
        mixed = attend(heads[None], (marks[None, :] | eye_windows)[None], HEAD)[0]
        update = jnp.einsum('whe,dhe->wd', mixed.astype(jnp.float32), global_table)
        result = (rows.astype(jnp.float32) + update).astype(jnp.bfloat16)
        return jnp.where(marks[:, None], result, jnp.zeros_like(result))
    encoded = lax.map(one_position, (by_position, present_by_position))
    return jnp.transpose(encoded, (1, 0, 2))
```

```python
import functools

import jax
import jax.numpy as jnp
from jax import lax
from jax.experimental import pallas as pl
from jax.experimental.pallas import tpu as pltpu
from jax.sharding import PartitionSpec as P

EPSILON = 1e-05


def normed(values, gain):
    floats = values.astype(jnp.float32)
    center = floats - jnp.mean(floats, axis=-1, keepdims=True)
    spread = jnp.mean(center * center, axis=-1, keepdims=True)
    return (center * lax.rsqrt(spread + EPSILON) * gain).astype(jnp.bfloat16)


def local_attend(heads, allowed, width):
    queries, key_part, value_part = (
        heads[..., :width],
        heads[..., width : 2 * width],
        heads[..., 2 * width :],
    )
    scores = jnp.einsum(
        "gqe,gke->gqk", queries, key_part, preferred_element_type=jnp.float32
    ) * width ** (-0.5)
    scores = jnp.where(allowed, scores, -jnp.inf)
    top = jnp.max(scores, axis=-1, keepdims=True)
    weights = jnp.exp(scores - top)
    weights = (weights / jnp.sum(weights, axis=-1, keepdims=True)).astype(jnp.bfloat16)
    return jnp.einsum("gqk,gke->gqe", weights, value_part, preferred_element_type=jnp.float32).astype(
        jnp.bfloat16
    )


def global_kernel(query_ref, pairs_ref, place_ref, ident_ref, codes_ref, out_ref):
    width = query_ref.shape[1]
    contract = (((1,), (1,)), ((), ()))
    scores = lax.dot_general(
        query_ref[...], pairs_ref[:, :width], contract, preferred_element_type=jnp.float32
    ) * width ** (-0.5)
    columns = lax.broadcasted_iota(jnp.int32, scores.shape, 1)
    allowed = (place_ref[...] == codes_ref[...]) | (ident_ref[...] == columns)
    scores = jnp.where(allowed, scores, -jnp.inf)
    top = jnp.max(scores, axis=-1, keepdims=True)
    weights = jnp.exp(scores - top)
    weights = (weights / jnp.sum(weights, axis=-1, keepdims=True)).astype(jnp.bfloat16)
    out_ref[...] = jnp.dot(
        weights, pairs_ref[:, width:], preferred_element_type=jnp.float32
    ).astype(out_ref.dtype)


def global_attend(query, pairs, place, ident, codes, tile):
    rows, width = query.shape
    keys = pairs.shape[0]
    return pl.pallas_call(
        global_kernel,
        grid=(rows // tile,),
        in_specs=[
            pl.BlockSpec((tile, width), lambda i: (i, 0)),
            pl.BlockSpec((keys, 2 * width), lambda i: (0, 0)),
            pl.BlockSpec((tile, 1), lambda i: (i, 0)),
            pl.BlockSpec((tile, 1), lambda i: (i, 0)),
            pl.BlockSpec((1, keys), lambda i: (0, 0)),
        ],
        out_specs=pl.BlockSpec((tile, width), lambda i: (i, 0)),
        out_shape=jax.ShapeDtypeStruct((rows, width), query.dtype),
        name="global_attend",
    )(query, pairs, place, ident, codes)


def after(value, *others):
    return lax.optimization_barrier((value, *others))[0]


def shards(
    patches,
    keep_lists,
    visible_counts,
    embed_weight,
    position_table,
    local_gain,
    local_projection,
    local_output,
    global_gain,
    global_projection,
    global_output,
):
    windows_here, slots = keep_lists.shape
    window_cells, width = position_table.shape
    heads_here = local_projection.shape[1]
    head = local_projection.shape[2] // 3
    seq_count = lax.axis_size("seq")
    tensor_count = lax.axis_size("tensor")
    share = width // tensor_count
    depth = heads_here
    across = seq_count // depth
    assert depth == 4 and tensor_count == 4 and across * depth == seq_count
    rows_here = windows_here * slots
    all_rows = depth * rows_here
    block = local_projection.shape[0]
    patch_in = patches.shape[1]
    quarter = rows_here // tensor_count
    s = lax.axis_index("seq")
    t = lax.axis_index("tensor")
    z = s // across
    x = s % across

    def swap_z(value, k):
        return lax.ppermute(
            value,
            "seq",
            [(a * across + b, (a ^ k) * across + b) for a in range(depth) for b in range(across)],
        )

    def swap_t(value, k):
        return lax.ppermute(value, "tensor", [(a, a ^ k) for a in range(tensor_count)])

    def from_x(value):
        if across == 2:
            other = lax.ppermute(value, "seq", [(a, a ^ 1) for a in range(seq_count)])
            return jnp.stack([value, other]), 0
        groups = [[a * across + b for b in range(across)] for a in range(depth)]
        return lax.all_gather(value, "seq", axis=0, axis_index_groups=groups), x

    def in_order_x(value):
        if across == 2:
            other = lax.ppermute(value, "seq", [(a, a ^ 1) for a in range(seq_count)])
            first = x == 0
            return jnp.stack([jnp.where(first, value, other), jnp.where(first, other, value)])
        return from_x(value)[0]

    def pick(stacked, index, axis=0):
        return lax.dynamic_index_in_dim(stacked, index, axis, keepdims=False)

    def head_rows(projection, tie):
        by_head = jnp.transpose(projection, (1, 0, 2))
        if tie is not None:
            by_head = after(by_head, tie)
        came = [pick(by_head, z)] + [swap_z(pick(by_head, z ^ k), k) for k in range(1, depth)]
        placed = jnp.zeros((depth, across, block, 3 * head), projection.dtype)
        for k in range(depth):
            placed = lax.dynamic_update_slice(
                placed, in_order_x(came[k])[None], (z ^ k, 0, 0, 0)
            )
        return placed.reshape(width, 3 * head), came[-1]

    def whole_table(table, tie):
        if tie is not None:
            table = after(table, tie)
        came = [table] + [swap_z(table, k) for k in range(1, depth)]
        placed = jnp.zeros((depth, across) + table.shape, table.dtype)
        for k in range(depth):
            placed = lax.dynamic_update_slice(
                placed, in_order_x(came[k])[None], (z ^ k, 0, 0, 0)
            )
        return placed.reshape(tensor_count, share, table.shape[1]), came[-1]

    offsets = jnp.arange(windows_here, dtype=jnp.int32)[:, None] * window_cells
    picked = patches[(keep_lists + offsets).reshape(-1)]
    notes = jnp.concatenate([keep_lists.reshape(-1), visible_counts]).astype(jnp.bfloat16)
    notes = jnp.pad(notes[None], ((0, 15), (0, patch_in - notes.shape[0])))
    message = jnp.concatenate(
        [lax.dynamic_slice_in_dim(picked, t * quarter, quarter, 0), notes], axis=0
    )
    came = [swap_z(message, k) for k in range(1, depth)]
    remote = jnp.stack([m[:quarter] for m in came])
    remote_y = swap_t(remote, 2)
    both = jnp.stack([remote, remote_y])
    both_c = swap_t(both, 1)
    by_t = jnp.stack([both[0], both_c[0], both[1], both_c[1]])
    far = jnp.stack([pick(by_t, t ^ k) for k in range(tensor_count)], axis=1)
    tiles = jnp.concatenate([picked, far.reshape((depth - 1) * rows_here, patch_in)], axis=0)
    facts = jnp.stack([notes[0]] + [m[quarter] for m in came]).astype(jnp.float32)
    keep = facts[:, :rows_here].astype(jnp.int32)
    counts = facts[:, rows_here : rows_here + windows_here].astype(jnp.int32)
    windows_held = depth * windows_here
    slot_ids = jnp.arange(slots, dtype=jnp.int32)
    visible = slot_ids[None, :] < counts.reshape(windows_held, 1)
    codes = jnp.where(visible, keep.reshape(windows_held, slots), -1)

    local_full, tie = head_rows(local_projection, None)
    local_back, tie = whole_table(local_output, tie)
    global_full, tie = head_rows(global_projection, tie)

    cell_ids = jnp.arange(window_cells, dtype=jnp.int32)
    hot = (keep.reshape(-1)[:, None] == cell_ids[None, :]).astype(jnp.bfloat16)
    embedded = jnp.dot(
        jnp.concatenate([tiles, hot], axis=1),
        jnp.concatenate([embed_weight, position_table], axis=0),
        preferred_element_type=jnp.float32,
    )
    start = embedded.astype(jnp.bfloat16)
    allowed = visible[:, None, :] | jnp.eye(slots, dtype=bool)[None]
    local_heads = jnp.dot(
        normed(start, local_gain), local_full, preferred_element_type=jnp.float32
    ).astype(jnp.bfloat16)
    local_mixed = local_attend(
        local_heads.reshape(windows_held, slots, 3 * head), allowed, head
    ).reshape(depth, rows_here, head)

    def project_back(mixed, table, residual):
        got = jnp.stack([mixed[0]] + [swap_z(mixed[k], k) for k in range(1, depth)])
        row = jnp.concatenate([pick(got, z ^ k) for k in range(depth)], axis=1)
        partial = jnp.einsum("rc,tdc->trd", row, table, preferred_element_type=jnp.float32)
        partial = partial.reshape(2, 2, rows_here, share)
        low, high = t & 1, t >> 1
        half = pick(partial, low, 1) + swap_t(pick(partial, 1 - low, 1), 1)
        total = pick(half, high) + swap_t(pick(half, 1 - high).astype(jnp.bfloat16), 2).astype(
            jnp.float32
        )
        return (residual.astype(jnp.float32) + total).astype(jnp.bfloat16)

    start_here = lax.dynamic_slice(start, (0, t * share), (rows_here, share))
    after_local = project_back(local_mixed, local_back, start_here)

    pieces = [after_local] + [swap_z(after_local, k) for k in range(1, depth)]
    heads = []
    for piece in pieces:
        piece_y = swap_t(piece, 2)
        pair = jnp.stack([piece, piece_y])
        pair_c = swap_t(pair, 1)
        by_t = jnp.stack([pair[0], pair_c[0], pair[1], pair_c[1]])
        rows = jnp.concatenate([pick(by_t, t ^ k) for k in range(tensor_count)], axis=1)
        heads.append(
            jnp.dot(
                normed(rows, global_gain), global_full, preferred_element_type=jnp.float32
            ).astype(jnp.bfloat16)
        )
    global_back, tie = whole_table(global_output, pieces[-1])
    global_heads = jnp.concatenate(heads, axis=0)
    pairs, spot = from_x(global_heads[:, head:])
    every_code, _ = from_x(codes)
    ident = spot * all_rows + jnp.arange(all_rows, dtype=jnp.int32)[:, None]
    global_mixed = global_attend(
        global_heads[:, :head],
        pairs.reshape(across * all_rows, 2 * head),
        keep.reshape(all_rows, 1),
        ident,
        every_code.reshape(1, across * all_rows),
        256 // across,
    ).reshape(depth, rows_here, head)
    encoded = project_back(global_mixed, global_back, after_local)
    own_codes = codes[:windows_here]
    cells_each = window_cells // seq_count
    cells = cell_ids.reshape(seq_count, 1, cells_each, 1)
    spread_hot = (own_codes[None, :, None, :] == cells).astype(jnp.bfloat16)
    spread = jnp.einsum(
        "swpj,wjd->swpd",
        spread_hot,
        encoded.reshape(windows_here, slots, share),
        preferred_element_type=jnp.float32,
    ).astype(jnp.bfloat16)
    result = lax.all_to_all(spread, "seq", split_axis=0, concat_axis=0, tiled=True)
    return result.reshape(seq_count * windows_here, cells_each, share)


def solution(mesh):
    placed = (
        P("seq", None),
        P("seq", None),
        P("seq"),
        P(),
        P(),
        P(),
        P("seq", "tensor", None),
        P("seq", "tensor"),
        P(),
        P("seq", "tensor", None),
        P("seq", "tensor"),
    )
    return jax.shard_map(
        shards, mesh=mesh, in_specs=placed, out_specs=P(None, "seq", "tensor"), check_vma=False
    )
```

```python
import functools

import jax
import jax.numpy as jnp
from jax import lax
from jax.experimental import pallas as pl
from jax.experimental.pallas import tpu as pltpu
from jax.sharding import PartitionSpec as P

EPSILON = 1e-05


def normed(values, gain):
    floats = values.astype(jnp.float32)
    center = floats - jnp.mean(floats, axis=-1, keepdims=True)
    spread = jnp.mean(center * center, axis=-1, keepdims=True)
    return (center * lax.rsqrt(spread + EPSILON) * gain).astype(jnp.bfloat16)


def local_attend(heads, allowed, width):
    queries, key_part, value_part = (
        heads[..., :width],
        heads[..., width : 2 * width],
        heads[..., 2 * width :],
    )
    scores = jnp.einsum(
        "gqe,gke->gqk", queries, key_part, preferred_element_type=jnp.float32
    ) * width ** (-0.5)
    scores = jnp.where(allowed, scores, -jnp.inf)
    top = jnp.max(scores, axis=-1, keepdims=True)
    weights = jnp.exp(scores - top)
    weights = (weights / jnp.sum(weights, axis=-1, keepdims=True)).astype(jnp.bfloat16)
    return jnp.einsum("gqk,gke->gqe", weights, value_part, preferred_element_type=jnp.float32).astype(
        jnp.bfloat16
    )


def global_kernel(query_ref, pairs_ref, place_ref, ident_ref, codes_ref, out_ref):
    width = query_ref.shape[1]
    contract = (((1,), (1,)), ((), ()))
    scores = lax.dot_general(
        query_ref[...], pairs_ref[:, :width], contract, preferred_element_type=jnp.float32
    ) * width ** (-0.5)
    columns = lax.broadcasted_iota(jnp.int32, scores.shape, 1)
    allowed = (place_ref[...] == codes_ref[...]) | (ident_ref[...] == columns)
    scores = jnp.where(allowed, scores, -jnp.inf)
    top = jnp.max(scores, axis=-1, keepdims=True)
    weights = jnp.exp(scores - top)
    total = jnp.sum(weights, axis=-1, keepdims=True)
    mixed = jnp.dot(
        weights.astype(jnp.bfloat16), pairs_ref[:, width:], preferred_element_type=jnp.float32
    )
    out_ref[...] = (mixed / total).astype(out_ref.dtype)


def global_attend(query, pairs, place, ident, codes, tile):
    rows, width = query.shape
    keys = pairs.shape[0]
    return pl.pallas_call(
        global_kernel,
        grid=(rows // tile,),
        in_specs=[
            pl.BlockSpec((tile, width), lambda i: (i, 0)),
            pl.BlockSpec((keys, 2 * width), lambda i: (0, 0)),
            pl.BlockSpec((tile, 1), lambda i: (i, 0)),
            pl.BlockSpec((tile, 1), lambda i: (i, 0)),
            pl.BlockSpec((1, keys), lambda i: (0, 0)),
        ],
        out_specs=pl.BlockSpec((tile, width), lambda i: (i, 0)),
        out_shape=jax.ShapeDtypeStruct((rows, width), query.dtype),
        name="global_attend",
    )(query, pairs, place, ident, codes)


def rows_kernel(spots_ref, near0, far0, near1, far1, gains_ref, table_ref, out_ref):
    own = spots_ref[2]
    floats = [ref[...].astype(jnp.float32) for ref in (near0, far0, near1, far1)]
    count = sum(f.shape[1] for f in floats)
    mean = sum(jnp.sum(f, axis=-1, keepdims=True) for f in floats) / count
    floats = [f - mean for f in floats]
    spread = sum(jnp.sum(f * f, axis=-1, keepdims=True) for f in floats) / count
    scale = lax.rsqrt(spread + EPSILON)
    total = None
    for i, f in enumerate(floats):
        part = 2 * (i // 2) + (own if i % 2 == 0 else 1 - own)
        ready = (f * scale * gains_ref[part]).astype(jnp.bfloat16)
        product = jnp.dot(ready, table_ref[part], preferred_element_type=jnp.float32)
        total = product if total is None else total + product
    out_ref[...] = total.astype(out_ref.dtype)


def project_rows(spots, near, far, gains, table):
    rows, share = near.shape[1:]
    columns = table.shape[2]

    def piece(high):
        def at(i, spots_ref):
            plane = spots_ref[0] ^ high
            return (2 * plane + (i ^ plane ^ spots_ref[1]), 0, 0)

        return pl.BlockSpec((None, rows, share), at)

    return pl.pallas_call(
        rows_kernel,
        grid_spec=pltpu.PrefetchScalarGridSpec(
            num_scalar_prefetch=1,
            grid=(2,),
            in_specs=[
                piece(0),
                piece(0),
                piece(1),
                piece(1),
                pl.BlockSpec(gains.shape, lambda i, spots_ref: (0, 0, 0)),
                pl.BlockSpec(table.shape, lambda i, spots_ref: (0, 0, 0)),
            ],
            out_specs=pl.BlockSpec((rows, columns), lambda i, spots_ref: (i, 0)),
        ),
        out_shape=jax.ShapeDtypeStruct((2 * rows, columns), near.dtype),
        name="project_rows",
    )(spots, near, far, near, far, gains, table)


def after(value, *others):
    return lax.optimization_barrier((value, *others))[0]


def shards(
    patches,
    keep_lists,
    visible_counts,
    embed_weight,
    position_table,
    local_gain,
    local_projection,
    local_output,
    global_gain,
    global_projection,
    global_output,
):
    windows_here, slots = keep_lists.shape
    window_cells, width = position_table.shape
    heads_here = local_projection.shape[1]
    head = local_projection.shape[2] // 3
    seq_count = lax.axis_size("seq")
    tensor_count = lax.axis_size("tensor")
    share = width // tensor_count
    depth = heads_here
    across = seq_count // depth
    assert depth == 4 and tensor_count == 4 and across * depth == seq_count
    rows_here = windows_here * slots
    all_rows = depth * rows_here
    block = local_projection.shape[0]
    patch_in = patches.shape[1]
    quarter = rows_here // tensor_count
    s = lax.axis_index("seq")
    t = lax.axis_index("tensor")
    z = s // across
    x = s % across

    def swap_z(value, k):
        return lax.ppermute(
            value,
            "seq",
            [(a * across + b, (a ^ k) * across + b) for a in range(depth) for b in range(across)],
        )

    def swap_t(value, k):
        return lax.ppermute(value, "tensor", [(a, a ^ k) for a in range(tensor_count)])

    def from_x(value):
        if across == 2:
            other = lax.ppermute(value, "seq", [(a, a ^ 1) for a in range(seq_count)])
            return jnp.stack([value, other]), 0
        groups = [[a * across + b for b in range(across)] for a in range(depth)]
        return lax.all_gather(value, "seq", axis=0, axis_index_groups=groups), x

    def in_order_x(value):
        if across == 2:
            other = lax.ppermute(value, "seq", [(a, a ^ 1) for a in range(seq_count)])
            first = x == 0
            return jnp.stack([jnp.where(first, value, other), jnp.where(first, other, value)])
        return from_x(value)[0]

    def pick(stacked, index, axis=0):
        return lax.dynamic_index_in_dim(stacked, index, axis, keepdims=False)

    def place(pieces, order):
        shape = (len(pieces),) + pieces[0].shape
        placed = jnp.zeros(shape, pieces[0].dtype)
        for piece, at in zip(pieces, order, strict=True):
            placed = lax.dynamic_update_slice(placed, piece[None], (at,) + (0,) * (len(shape) - 1))
        return placed.reshape(shape[0], shape[1] * shape[2], shape[3])

    def send_heads(by_head):
        return [pick(by_head, z)] + [swap_z(pick(by_head, z ^ k), k) for k in range(1, depth)]

    natural = [z ^ k for k in range(depth)]

    offsets = jnp.arange(windows_here, dtype=jnp.int32)[:, None] * window_cells
    picked = patches[(keep_lists + offsets).reshape(-1)]
    notes = jnp.concatenate([keep_lists.reshape(-1), visible_counts]).astype(jnp.bfloat16)
    notes = jnp.pad(notes[None], ((0, 15), (0, patch_in - notes.shape[0])))
    message = jnp.concatenate(
        [lax.dynamic_slice_in_dim(picked, t * quarter, quarter, 0), notes], axis=0
    )
    came = [swap_z(message, k) for k in range(1, depth)]
    remote = jnp.stack([m[:quarter] for m in came])
    remote_y = swap_t(remote, 2)
    both = jnp.stack([remote, remote_y])
    both_c = swap_t(both, 1)
    by_t = jnp.stack([both[0], both_c[0], both[1], both_c[1]])
    far = jnp.stack([pick(by_t, t ^ k) for k in range(tensor_count)], axis=1)
    tiles = jnp.concatenate([picked, far.reshape((depth - 1) * rows_here, patch_in)], axis=0)
    facts = jnp.stack([notes[0]] + [m[quarter] for m in came]).astype(jnp.float32)
    keep = facts[:, :rows_here].astype(jnp.int32)
    counts = facts[:, rows_here : rows_here + windows_here].astype(jnp.int32)
    windows_held = depth * windows_here
    slot_ids = jnp.arange(slots, dtype=jnp.int32)
    visible = slot_ids[None, :] < counts.reshape(windows_held, 1)
    codes = jnp.where(visible, keep.reshape(windows_held, slots), -1)

    sent = send_heads(jnp.transpose(local_projection, (1, 0, 2)))
    sent_x = [in_order_x(sent[0]), in_order_x(after(sent[1], came[-1]))]
    sent_x += [in_order_x(after(piece, both_c)) for piece in sent[2:]]
    local_full = place(sent_x, natural).reshape(width, 3 * head)
    back = after(local_output, came[-1])
    back_z = swap_z(back, 1)
    back_x = in_order_x(back)
    far_sent = send_heads(after(jnp.transpose(global_projection, (1, 0, 2)), both_c))
    far_x = in_order_x(far_sent[0])

    cell_ids = jnp.arange(window_cells, dtype=jnp.int32)
    hot = (keep.reshape(-1)[:, None] == cell_ids[None, :]).astype(jnp.bfloat16)
    embedded = jnp.dot(
        jnp.concatenate([tiles, hot], axis=1),
        jnp.concatenate([embed_weight, position_table], axis=0),
        preferred_element_type=jnp.float32,
    )
    start = embedded.astype(jnp.bfloat16)
    allowed = visible[:, None, :] | jnp.eye(slots, dtype=bool)[None]
    local_heads = jnp.dot(
        normed(start, local_gain), local_full, preferred_element_type=jnp.float32
    ).astype(jnp.bfloat16)
    local_mixed = local_attend(
        local_heads.reshape(windows_held, slots, 3 * head), allowed, head
    ).reshape(depth, rows_here, head)

    local_back = place([back_x, in_order_x(after(back_z, local_heads))], [z & 1, 1 - (z & 1)])
    sent_x = [far_x] + [in_order_x(after(piece, local_mixed)) for piece in far_sent[1:]]
    global_full = place(sent_x, natural)
    low, high = t & 1, t >> 1

    def gather_sum(partial):
        half = pick(partial, low, 1) + swap_t(pick(partial, 1 - low, 1), 1)
        return pick(half, high) + swap_t(pick(half, 1 - high).astype(jnp.bfloat16), 2).astype(
            jnp.float32
        )

    got = [jnp.stack([local_mixed[k], local_mixed[k ^ 2]]) for k in range(depth)]
    got = jnp.stack([got[0]] + [swap_z(got[k], k) for k in range(1, depth)])
    row = jnp.concatenate([pick(got, z ^ k) for k in range(depth)], axis=-1)
    partial = jnp.einsum("jrc,qdc->jqrd", row, local_back, preferred_element_type=jnp.float32)
    start_here = lax.dynamic_slice(
        start,
        (2 * high * rows_here, (2 * (z >> 1) + low) * share),
        (rows_here, share),
    )
    after_local = (start_here.astype(jnp.float32) + gather_sum(partial)).astype(jnp.bfloat16)

    spots = jnp.stack([z >> 1, high, low]).astype(jnp.int32)
    gains = global_gain.reshape(tensor_count, 1, share)
    pieces = [after_local] + [swap_z(after_local, k) for k in range(1, depth)]
    pieces_y = [swap_t(piece, 2) for piece in pieces]
    heads, pairs = [], []
    near = jnp.stack([pieces[0], pieces_y[0], pieces[2], pieces_y[2]])
    far_parts = swap_t(near, 1)
    grouped = [(near, far_parts)]
    near1 = jnp.stack([pieces[1], pieces_y[1]])
    near3 = jnp.stack([pieces[3], pieces_y[3]])
    grouped.append(
        (
            jnp.concatenate([near1, near3]),
            jnp.concatenate([swap_t(near1, 1), swap_t(near3, 1)]),
        )
    )
    for near, far in grouped:
        heads.append(project_rows(spots, near, far, gains, global_full))
        pairs.append(from_x(heads[-1][:, head:])[0])
    spot = 0 if across == 2 else x
    pairs = jnp.concatenate(pairs, axis=1)
    turn = (0, 2, 1, 3)
    global_heads = jnp.concatenate(heads, axis=0)
    place_here = jnp.stack([keep[k] for k in turn]).reshape(all_rows, 1)
    codes_by_z = codes.reshape(depth, rows_here)
    every_code = from_x(jnp.stack([codes_by_z[k] for k in turn]).reshape(all_rows))[0]
    ident = spot * all_rows + jnp.arange(all_rows, dtype=jnp.int32)[:, None]
    global_mixed = global_attend(
        global_heads[:, :head],
        pairs.reshape(across * all_rows, 2 * head),
        place_here,
        ident,
        every_code.reshape(1, across * all_rows),
        256 // across,
    ).reshape(depth, rows_here, head)
    global_mixed = [global_mixed[k] for k in turn]

    table = after(global_output, pieces[3])
    table_z = [table] + [swap_z(table, k) for k in range(1, depth)]
    table_x = [in_order_x(table)] + [in_order_x(after(piece, pairs)) for piece in table_z[1:]]
    global_back = place(table_x, natural)
    got = jnp.stack([global_mixed[0]] + [swap_z(global_mixed[k], k) for k in range(1, depth)])
    row = jnp.concatenate([pick(got, z ^ k) for k in range(depth)], axis=-1)
    partial = jnp.einsum("rc,tdc->trd", row, global_back, preferred_element_type=jnp.float32)
    plane = (z >> 1) ^ high
    held = 2 * plane + (plane ^ high)
    residual = pick(grouped[0][0], held)
    total = gather_sum(partial.reshape(2, 2, rows_here, share))
    encoded = (residual.astype(jnp.float32) + total).astype(jnp.bfloat16)
    own_codes = codes[:windows_here]
    cells_each = window_cells // seq_count
    cells = cell_ids.reshape(seq_count, 1, cells_each, 1)
    spread_hot = (own_codes[None, :, None, :] == cells).astype(jnp.bfloat16)
    spread = jnp.einsum(
        "swpj,wjd->swpd",
        spread_hot,
        encoded.reshape(windows_here, slots, share),
        preferred_element_type=jnp.float32,
    ).astype(jnp.bfloat16)
    result = lax.all_to_all(spread, "seq", split_axis=0, concat_axis=0, tiled=True)
    return result.reshape(seq_count * windows_here, cells_each, share)


def solution(mesh):
    placed = (
        P("seq", None),
        P("seq", None),
        P("seq"),
        P(),
        P(),
        P(),
        P("seq", "tensor", None),
        P("seq", "tensor"),
        P(),
        P("seq", "tensor", None),
        P("seq", "tensor"),
    )
    return jax.shard_map(
        shards, mesh=mesh, in_specs=placed, out_specs=P(None, "seq", "tensor"), check_vma=False
    )
```

```python
import functools
import math

import jax
import jax.numpy as jnp
from jax import lax
from jax.experimental import pallas as pl
from jax.experimental.pallas import tpu as pltpu
from jax.sharding import PartitionSpec as P


EPSILON = 1e-05


def normed(values, gain):
    floats = values.astype(jnp.float32)
    center = floats - jnp.mean(floats, axis=-1, keepdims=True)
    spread = jnp.mean(center * center, axis=-1, keepdims=True)
    return (center * lax.rsqrt(spread + EPSILON) * gain).astype(jnp.bfloat16)


def local_attend(heads, allowed, width):
    queries, key_part, value_part = (
        heads[..., :width],
        heads[..., width : 2 * width],
        heads[..., 2 * width :],
    )
    scores = jnp.einsum(
        "gqe,gke->gqk", queries, key_part, preferred_element_type=jnp.float32
    ) * width ** (-0.5)
    scores = jnp.where(allowed, scores, -jnp.inf)
    top = jnp.max(scores, axis=-1, keepdims=True)
    weights = jnp.exp(scores - top)
    weights = (weights / jnp.sum(weights, axis=-1, keepdims=True)).astype(jnp.bfloat16)
    return jnp.einsum("gqk,gke->gqe", weights, value_part, preferred_element_type=jnp.float32).astype(
        jnp.bfloat16
    )


def global_kernel(own_ref, query_a, query_b, place_ref, codes_ref, heads_a, heads_b, *refs):
    *pair_refs, out_ref = refs
    tile, width = out_ref.shape
    step, half = pl.program_id(0), pl.num_programs(0) // 2
    query = jnp.where(step < half, query_a[...], query_b[...])
    contract = (((1,), (1,)), ((), ()))
    apart = len(pair_refs) == 2
    blocks = [(ref, width, width * 2, True) for ref in (heads_a, heads_b)] if apart else []
    blocks += [(ref, 0, width, not apart) for ref in pair_refs]
    ident = own_ref[0] + step * tile + lax.broadcasted_iota(jnp.int32, (tile, 1), 0)
    parts, begin = [], 0
    for ref, key, _, own in blocks:
        keys = ref.shape[0]
        scores = lax.dot_general(
            query, ref[:, key : key + width], contract, preferred_element_type=jnp.float32
        )
        allowed = place_ref[...] == codes_ref[:, begin : begin + keys]
        if own:
            columns = lax.broadcasted_iota(jnp.int32, scores.shape, 1) + begin
            allowed = allowed | (ident == columns)
        parts.append(jnp.where(allowed, scores, -jnp.inf))
        begin += keys
    top = functools.reduce(jnp.maximum, [jnp.max(p, axis=-1, keepdims=True) for p in parts])
    total, mixed = 0.0, 0.0
    factor = width ** (-0.5) * math.log2(math.e)
    for (ref, _, value, _), scores in zip(blocks, parts, strict=True):
        weights = jnp.exp2((scores - top) * factor)
        total = total + jnp.sum(weights, axis=-1, keepdims=True)
        mixed = mixed + jnp.dot(
            weights.astype(jnp.bfloat16),
            ref[:, value : value + width],
            preferred_element_type=jnp.float32,
        )
    out_ref[...] = (mixed / total).astype(out_ref.dtype)


def global_attend(own, place, codes, heads_a, heads_b, pairs, tile):
    rows = heads_a.shape[0]
    width = heads_a.shape[1] // 3
    half = rows // tile
    whole = [heads_a, heads_b, *pairs]
    return pl.pallas_call(
        global_kernel,
        grid_spec=pltpu.PrefetchScalarGridSpec(
            num_scalar_prefetch=1,
            grid=(2 * half,),
            in_specs=[
                pl.BlockSpec((tile, width), lambda i, _: (jnp.minimum(i, half - 1), 0)),
                pl.BlockSpec((tile, width), lambda i, _: (jnp.maximum(i - half, 0), 0)),
                pl.BlockSpec((tile, 1), lambda i, _: (i, 0)),
                pl.BlockSpec(codes.shape, lambda i, _: (0, 0)),
            ]
            + [pl.BlockSpec(p.shape, lambda i, _: (0, 0)) for p in whole],
            out_specs=pl.BlockSpec((tile, width), lambda i, _: (i, 0)),
        ),
        out_shape=jax.ShapeDtypeStruct((2 * rows, width), heads_a.dtype),
        name="global_attend",
    )(own, heads_a, heads_b, place, codes, *whole)


def after(value, *others):
    return lax.optimization_barrier((value, *others))[0]


def shards(
    patches,
    keep_lists,
    visible_counts,
    embed_weight,
    position_table,
    local_gain,
    local_projection,
    local_output,
    global_gain,
    global_projection,
    global_output,
):
    windows_here, slots = keep_lists.shape
    window_cells, width = position_table.shape
    heads_here = local_projection.shape[1]
    head = local_projection.shape[2] // 3
    seq_count = lax.axis_size("seq")
    tensor_count = lax.axis_size("tensor")
    share = width // tensor_count
    depth = heads_here
    across = seq_count // depth
    assert depth == 4 and tensor_count == 4 and across * depth == seq_count
    rows_here = windows_here * slots
    all_rows = depth * rows_here
    patch_in = patches.shape[1]
    quarter = rows_here // tensor_count
    s = lax.axis_index("seq")
    t = lax.axis_index("tensor")
    z = s // across
    x = s % across

    def swap_z(value, k):
        return lax.ppermute(
            value,
            "seq",
            [(a * across + b, (a ^ k) * across + b) for a in range(depth) for b in range(across)],
        )

    def swap_t(value, k):
        return lax.ppermute(value, "tensor", [(a, a ^ k) for a in range(tensor_count)])

    def from_x(value):
        if across == 2:
            return [value, lax.ppermute(value, "seq", [(a, a ^ 1) for a in range(seq_count)])]
        groups = [[a * across + b for b in range(across)] for a in range(depth)]
        every = lax.all_gather(value, "seq", axis=0, axis_index_groups=groups)
        return [every[b] for b in range(across)]

    def pick(stacked, index, axis=0):
        return lax.dynamic_index_in_dim(stacked, index, axis, keepdims=False)

    def place(pieces, order, tie):
        pieces, _ = lax.optimization_barrier((pieces, tie))
        shape = (len(pieces), across) + pieces[0][0].shape
        placed = jnp.zeros(shape, pieces[0][0].dtype)
        spots = [x, 1 - x] if across == 2 else range(across)
        for every, at in zip(pieces, order, strict=True):
            for piece, spot in zip(every, spots, strict=True):
                placed = lax.dynamic_update_slice(placed, piece[None, None], (at, spot, 0, 0))
        return placed.reshape(shape[0], shape[1] * shape[2], shape[3])

    def send_heads(by_head):
        return [pick(by_head, z)] + [swap_z(pick(by_head, z ^ k), k) for k in range(1, depth)]

    natural = [z ^ k for k in range(depth)]

    offsets = jnp.arange(windows_here, dtype=jnp.int32)[:, None] * window_cells
    picked = patches[(keep_lists + offsets).reshape(-1)]
    notes = jnp.concatenate([keep_lists.reshape(-1), visible_counts]).astype(jnp.bfloat16)
    notes = jnp.pad(notes[None], ((0, 15), (0, patch_in - notes.shape[0])))
    message = jnp.concatenate(
        [lax.dynamic_slice_in_dim(picked, t * quarter, quarter, 0), notes], axis=0
    )
    came = [swap_z(message, k) for k in range(1, depth)]
    remote = jnp.stack(came)
    remote_y = swap_t(remote, 2)
    both = jnp.stack([remote, remote_y])
    both_c = swap_t(both, 1)
    by_t = jnp.stack([both[0], both_c[0], both[1], both_c[1]])
    far = jnp.stack([pick(by_t, t ^ k)[:, :quarter] for k in range(tensor_count)], axis=1)
    tiles = jnp.concatenate([picked, far.reshape((depth - 1) * rows_here, patch_in)], axis=0)
    facts = jnp.concatenate([notes[:1], after(remote, remote_y)[:, quarter]]).astype(jnp.float32)
    keep = facts[:, :rows_here].astype(jnp.int32)
    counts = facts[:, rows_here : rows_here + windows_here].astype(jnp.int32)
    windows_held = depth * windows_here
    slot_ids = jnp.arange(slots, dtype=jnp.int32)
    visible = slot_ids[None, :] < counts.reshape(windows_held, 1)
    codes = jnp.where(visible, keep.reshape(windows_held, slots), -1)

    sent = send_heads(jnp.transpose(local_projection, (1, 0, 2)))
    sent_x = [from_x(sent[k]) for k in range(depth)]
    head_x = sent_x
    back_z = swap_z(local_output, 1)
    back_x = [from_x(local_output)]
    sent = send_heads(jnp.transpose(after(global_projection, remote_y), (1, 0, 2)))
    far_x = [from_x(sent[k]) for k in range(depth)]
    table_z = [global_output] + [swap_z(global_output, k) for k in range(1, depth)]
    table_x = [from_x(table_z[k]) for k in range(depth)]

    cell_ids = jnp.arange(window_cells, dtype=jnp.int32)
    hot = (keep.reshape(-1)[:, None] == cell_ids[None, :]).astype(jnp.bfloat16)
    embedded = jnp.dot(
        jnp.concatenate([tiles, hot], axis=1),
        jnp.concatenate([embed_weight, position_table], axis=0),
        preferred_element_type=jnp.float32,
    )
    start = embedded.astype(jnp.bfloat16)
    back_x.append(from_x(after(back_z, start)))
    local_full = place(head_x, natural, start).reshape(width, 3 * head)
    allowed = visible[:, None, :] | jnp.eye(slots, dtype=bool)[None]
    local_heads = jnp.dot(
        normed(start, local_gain), local_full, preferred_element_type=jnp.float32
    ).astype(jnp.bfloat16)
    local_mixed = local_attend(
        local_heads.reshape(windows_held, slots, 3 * head), allowed, head
    ).reshape(depth, rows_here, head)

    low, high = t & 1, t >> 1

    def gather_sum(partial):
        half = pick(partial, low, 1) + swap_t(pick(partial, 1 - low, 1), 1)
        sent = pick(half, 1 - high).astype(jnp.bfloat16)
        return pick(half, high) + swap_t(sent, 2).astype(jnp.float32)

    got = [jnp.stack([local_mixed[k], local_mixed[k ^ 2]]) for k in range(depth)]
    got = jnp.stack([got[0]] + [swap_z(got[k], k) for k in range(1, depth)])
    row = jnp.concatenate([pick(got, z ^ k) for k in range(depth)], axis=-1)
    local_back = place(back_x, [z & 1, 1 - (z & 1)], local_mixed)
    partial = jnp.einsum("jrc,qdc->jqrd", row, local_back, preferred_element_type=jnp.float32)
    start_here = lax.dynamic_slice(
        start,
        (2 * high * rows_here, (2 * (z >> 1) + low) * share),
        (rows_here, share),
    )
    after_local = (start_here.astype(jnp.float32) + gather_sum(partial)).astype(jnp.bfloat16)

    pieces = [after_local] + [swap_z(after_local, k) for k in range(1, depth)]
    pieces_y = [swap_t(pieces[k], 2) for k in range(depth)]
    global_full = place(far_x, natural, pieces[1]).reshape(width, 3 * head)

    def project_rows(parts):
        every = jnp.concatenate(parts)
        heads = []
        for i in range(2):
            quarters = []
            for quarter in range(tensor_count):
                plane = (z >> 1) ^ (quarter >> 1)
                spot = 4 * (low ^ (quarter & 1)) + 2 * plane + (i ^ plane ^ high)
                quarters.append(pick(every, spot))
            rows = jnp.concatenate(quarters, axis=1)
            heads.append(
                jnp.dot(
                    normed(rows, global_gain), global_full, preferred_element_type=jnp.float32
                ).astype(jnp.bfloat16)
            )
        return jnp.concatenate(heads, axis=0)

    near = [jnp.stack([pieces[k], pieces_y[k]]) for k in range(depth)]
    far = [swap_t(near[k], 1) for k in range(depth)]
    heads_a = project_rows([near[0], near[2], far[0], far[2]])
    pairs = from_x(heads_a[:, head:])
    heads_b = project_rows([near[1], near[3], far[1], far[3]])
    pairs_b = from_x(heads_b[:, head:])
    pairs = [p for both in zip(pairs, pairs_b, strict=True) for p in both]
    turn = (0, 2, 1, 3)
    spot = 0 if across == 2 else x
    place_here = jnp.stack([keep[k] for k in turn]).reshape(all_rows, 1)
    codes_by_z = codes.reshape(depth, rows_here)
    every_code = from_x(jnp.stack([codes_by_z[k] for k in turn]).reshape(1, all_rows))
    own = jnp.full((1,), spot * all_rows, jnp.int32)
    if across == 2:
        pairs = pairs[2:]
    global_mixed = global_attend(
        own, place_here, jnp.concatenate(every_code, axis=1), heads_a, heads_b, pairs, 256 // across
    ).reshape(depth, rows_here, head)
    global_mixed = [global_mixed[k] for k in turn]

    got = jnp.stack([global_mixed[0]] + [swap_z(global_mixed[k], k) for k in range(1, depth)])
    row = jnp.concatenate([pick(got, z ^ k) for k in range(depth)], axis=-1)
    global_back = place(table_x, natural, global_mixed[0])
    partial = jnp.einsum("rc,tdc->trd", row, global_back, preferred_element_type=jnp.float32)
    plane = (z >> 1) ^ high
    held = 2 * plane + (plane ^ high)
    residual = pick(jnp.concatenate([near[0], near[2]]), held)
    total = gather_sum(partial.reshape(2, 2, rows_here, share))
    encoded = (residual.astype(jnp.float32) + total).astype(jnp.bfloat16)
    own_codes = codes[:windows_here]
    cells_each = window_cells // seq_count
    cells = cell_ids.reshape(seq_count, 1, cells_each, 1)
    spread_hot = (own_codes[None, :, None, :] == cells).astype(jnp.bfloat16)
    spread = jnp.einsum(
        "swpj,wjd->swpd",
        spread_hot,
        encoded.reshape(windows_here, slots, share),
        preferred_element_type=jnp.float32,
    ).astype(jnp.bfloat16)
    result = lax.all_to_all(spread, "seq", split_axis=0, concat_axis=0, tiled=True)
    return result.reshape(seq_count * windows_here, cells_each, share)


def solution(mesh):
    run = place_and_run(mesh)
    return run


def place_and_run(mesh):
    placed = (
        P("seq", None),
        P("seq", None),
        P("seq"),
        P(),
        P(),
        P(),
        P("seq", "tensor", None),
        P("seq", "tensor"),
        P(),
        P("seq", "tensor", None),
        P("seq", "tensor"),
    )

    return jax.shard_map(
        shards, mesh=mesh, in_specs=placed, out_specs=P(None, "seq", "tensor"), check_vma=False
    )
```

```python
import functools
import math

import jax
import jax.numpy as jnp
from jax import lax
from jax.experimental import pallas as pl
from jax.experimental.pallas import tpu as pltpu
from jax.sharding import PartitionSpec as P


EPSILON = 1e-05


def normed(values, gain):
    floats = values.astype(jnp.float32)
    center = floats - jnp.mean(floats, axis=-1, keepdims=True)
    spread = jnp.mean(center * center, axis=-1, keepdims=True)
    return (center * lax.rsqrt(spread + EPSILON) * gain).astype(jnp.bfloat16)


def local_attend(heads, allowed, width):
    queries, key_part, value_part = (
        heads[..., :width],
        heads[..., width : 2 * width],
        heads[..., 2 * width :],
    )
    scores = jnp.einsum(
        "gqe,gke->gqk", queries, key_part, preferred_element_type=jnp.float32
    ) * width ** (-0.5)
    scores = jnp.where(allowed, scores, -jnp.inf)
    top = jnp.max(scores, axis=-1, keepdims=True)
    weights = jnp.exp(scores - top)
    weights = (weights / jnp.sum(weights, axis=-1, keepdims=True)).astype(jnp.bfloat16)
    return jnp.einsum("gqk,gke->gqe", weights, value_part, preferred_element_type=jnp.float32).astype(
        jnp.bfloat16
    )


def scores_over(query, place, ident, codes_ref, pair_refs, own):
    width = query.shape[1]
    factor = width ** (-0.5) * math.log2(math.e)
    parts, begin = [], 0
    for ref in pair_refs:
        keys = ref.shape[0]
        scores = lax.dot_general(
            query, ref[:, :width], (((1,), (1,)), ((), ())), preferred_element_type=jnp.float32
        )
        allowed = place == codes_ref[:, begin : begin + keys]
        if own:
            columns = lax.broadcasted_iota(jnp.int32, scores.shape, 1) + begin
            allowed = allowed | (ident == columns)
        parts.append(jnp.where(allowed, scores, -jnp.inf))
        begin += keys
    top = functools.reduce(jnp.maximum, [jnp.max(p, axis=-1, keepdims=True) for p in parts])
    return parts, top, factor


def weigh(parts, top, factor, pair_refs, width):
    total, mixed = 0.0, 0.0
    for ref, scores in zip(pair_refs, parts, strict=True):
        weights = jnp.exp2((scores - top) * factor)
        total = total + jnp.sum(weights, axis=-1, keepdims=True)
        mixed = mixed + jnp.dot(
            weights.astype(jnp.bfloat16), ref[:, width:], preferred_element_type=jnp.float32
        )
    return total, mixed


def own_kernel(own_ref, query_a, query_b, place_ref, codes_ref, *refs):
    *pair_refs, top_ref, total_ref, mixed_ref = refs
    tile, width = mixed_ref.shape
    step, half = pl.program_id(0), pl.num_programs(0) // 2
    query = jnp.where(step < half, query_a[...], query_b[...])
    ident = own_ref[0] + step * tile + lax.broadcasted_iota(jnp.int32, (tile, 1), 0)
    parts, top, factor = scores_over(query, place_ref[...], ident, codes_ref, pair_refs, True)
    total, mixed = weigh(parts, top, factor, pair_refs, width)
    top_ref[...], total_ref[...], mixed_ref[...] = top, total, mixed


def rest_kernel(query_a, query_b, place_ref, codes_ref, top_ref, total_ref, mixed_ref, *refs):
    *pair_refs, out_ref = refs
    _, width = out_ref.shape
    step, half = pl.program_id(0), pl.num_programs(0) // 2
    query = jnp.where(step < half, query_a[...], query_b[...])
    parts, top, factor = scores_over(query, place_ref[...], None, codes_ref, pair_refs, False)
    before = top_ref[...]
    top = jnp.maximum(top, before)
    total, mixed = weigh(parts, top, factor, pair_refs, width)
    scale = jnp.exp2((before - top) * factor)
    total = total + total_ref[...] * scale
    out_ref[...] = ((mixed + mixed_ref[...] * scale) / total).astype(out_ref.dtype)


def global_attend(own, place, codes, query_a, query_b, pairs, tile):
    rows, width = query_a.shape
    half = rows // tile
    first = not isinstance(own, tuple)

    def by_tile(columns):
        return pl.BlockSpec((tile, columns), lambda i: (i, 0))

    specs = [
        pl.BlockSpec((tile, width), lambda i: (jnp.minimum(i, half - 1), 0)),
        pl.BlockSpec((tile, width), lambda i: (jnp.maximum(i - half, 0), 0)),
        by_tile(1),
        pl.BlockSpec(codes.shape, lambda i: (0, 0)),
    ]
    pair_specs = [pl.BlockSpec(p.shape, lambda i: (0, 0)) for p in pairs]
    kinds = [
        jax.ShapeDtypeStruct((2 * rows, columns), kind)
        for columns, kind in (
            ((1, jnp.float32), (1, jnp.float32), (width, jnp.float32))
            if first
            else ((width, query_a.dtype),)
        )
    ]
    if first:
        return pl.pallas_call(
            own_kernel,
            grid=(2 * half,),
            in_specs=[pl.BlockSpec(memory_space=pltpu.SMEM), *specs, *pair_specs],
            out_specs=[by_tile(1), by_tile(1), by_tile(width)],
            out_shape=kinds,
            name="own_attend",
        )(own, query_a, query_b, place, codes, *pairs)
    return pl.pallas_call(
        rest_kernel,
        grid=(2 * half,),
        in_specs=[*specs, by_tile(1), by_tile(1), by_tile(width), *pair_specs],
        out_specs=by_tile(width),
        out_shape=kinds[0],
        name="rest_attend",
    )(query_a, query_b, place, codes, *own, *pairs)


def fill(table_ref, piece_refs, spots_ref):
    parts = table_ref.shape[0]
    across = len(piece_refs) // parts
    for i, ref in enumerate(piece_refs):
        at, spot = spots_ref[i // across], spots_ref[parts + i % across]
        rows = ref.shape[0]
        table_ref[at, pl.ds(pl.multiple_of(spot * rows, rows), rows), :] = ref[...]


def whole_vmem(count):
    return [pl.BlockSpec(memory_space=pltpu.VMEM)] * count


def rows_kernel(bits_ref, spots_ref, gains_ref, *refs):
    *refs, query_ref, pair_ref, table_ref = refs
    own, own_y, far, far_y = refs[0:2], refs[2:4], refs[4:6], refs[6:8]
    fill(table_ref, refs[8:], spots_ref)
    upper, high, low = bits_ref[0], bits_ref[1], bits_ref[2]
    rows, width = own[0].shape[0], query_ref.shape[1]
    choices = (
        (high, (own[0], far[0], own_y[1], far_y[1])),
        (1 - high, (own_y[0], far_y[0], own[1], far[1])),
    )
    for row, parts in choices:
        floats = [ref[...].astype(jnp.float32) for ref in parts]
        count = sum(f.shape[1] for f in floats)
        mean = sum(jnp.sum(f, axis=-1, keepdims=True) for f in floats) / count
        floats = [f - mean for f in floats]
        spread = sum(jnp.sum(f * f, axis=-1, keepdims=True) for f in floats) / count
        total = None
        for i, f in enumerate(floats):
            half = upper if i < 2 else 1 - upper
            quarter = 2 * half + (low if i % 2 == 0 else 1 - low)
            ready = (f * gains_ref[quarter]).astype(jnp.bfloat16)
            product = jnp.dot(ready, table_ref[quarter], preferred_element_type=jnp.float32)
            total = product if total is None else total + product
        heads = (total * lax.rsqrt(spread + EPSILON)).astype(query_ref.dtype)
        begin = pl.multiple_of(row * rows, rows)
        query_ref[pl.ds(begin, rows), :] = heads[:, :width]
        pair_ref[pl.ds(begin, rows), :] = heads[:, width:]


def project_rows(bits, spots, gains, own, own_y, far, far_y, pieces, head):
    rows, share = own[0].shape
    operands = [*own, *own_y, *far, *far_y, *pieces]
    kind = own[0].dtype
    return pl.pallas_call(
        rows_kernel,
        in_specs=[pl.BlockSpec(memory_space=pltpu.SMEM)] * 2 + whole_vmem(1 + len(operands)),
        out_specs=whole_vmem(2),
        out_shape=[
            jax.ShapeDtypeStruct((2 * rows, head), kind),
            jax.ShapeDtypeStruct((2 * rows, 2 * head), kind),
        ],
        scratch_shapes=[pltpu.VMEM((gains.shape[0], share, 3 * head), kind)],
        name="project_rows",
    )(bits, spots, gains, *operands)


def back_kernel(bits_ref, spots_ref, *refs):
    *refs, keep_ref, send_ref, row_ref, table_ref = refs
    depth = row_ref.shape[2] // refs[0].shape[2]
    fill(table_ref, refs[depth:], spots_ref)
    low, head = bits_ref[2], refs[0].shape[2]
    for k in range(depth):
        begin = pl.multiple_of(bits_ref[3 + k] * head, head)
        row_ref[:, :, pl.ds(begin, head)] = refs[k][...]
    contract = (((1,), (1,)), ((), ()))
    apart = row_ref.shape[0] == 2
    for i in range(2):
        row = row_ref[i if apart else 0]
        keep, send = (low, 1 - low) if apart else (2 * i + low, 2 * i + 1 - low)
        keep_ref[i] = lax.dot_general(
            row, table_ref[keep], contract, preferred_element_type=jnp.float32
        )
        send_ref[i] = lax.dot_general(
            row, table_ref[send], contract, preferred_element_type=jnp.float32
        ).astype(send_ref.dtype)


def project_back(bits, spots, mixed, pieces, parts, share):
    groups, rows, head = mixed[0].shape
    kind = mixed[0].dtype
    width = len(mixed) * head
    return pl.pallas_call(
        back_kernel,
        in_specs=[pl.BlockSpec(memory_space=pltpu.SMEM)] * 2
        + whole_vmem(len(mixed) + len(pieces)),
        out_specs=whole_vmem(2),
        out_shape=[
            jax.ShapeDtypeStruct((2, rows, share), jnp.float32),
            jax.ShapeDtypeStruct((2, rows, share), kind),
        ],
        scratch_shapes=[
            pltpu.VMEM((groups, rows, width), kind),
            pltpu.VMEM((parts, share, width), kind),
        ],
        name="project_back",
    )(bits, spots, *mixed, *pieces)


def after(value, *others):
    return lax.optimization_barrier((value, *others))[0]


def shards(
    patches,
    keep_lists,
    visible_counts,
    embed_weight,
    position_table,
    local_gain,
    local_projection,
    local_output,
    global_gain,
    global_projection,
    global_output,
):
    windows_here, slots = keep_lists.shape
    window_cells, width = position_table.shape
    heads_here = local_projection.shape[1]
    head = local_projection.shape[2] // 3
    seq_count = lax.axis_size("seq")
    tensor_count = lax.axis_size("tensor")
    share = width // tensor_count
    depth = heads_here
    across = seq_count // depth
    assert depth == 4 and tensor_count == 4 and across * depth == seq_count
    rows_here = windows_here * slots
    all_rows = depth * rows_here
    patch_in = patches.shape[1]
    quarter = rows_here // tensor_count
    s = lax.axis_index("seq")
    t = lax.axis_index("tensor")
    z = s // across
    x = s % across

    def swap_z(value, k):
        return lax.ppermute(
            value,
            "seq",
            [(a * across + b, (a ^ k) * across + b) for a in range(depth) for b in range(across)],
        )

    def swap_t(value, k):
        return lax.ppermute(value, "tensor", [(a, a ^ k) for a in range(tensor_count)])

    def from_x(value):
        if across == 2:
            return [value, lax.ppermute(value, "seq", [(a, a ^ 1) for a in range(seq_count)])]
        groups = [[a * across + b for b in range(across)] for a in range(depth)]
        every = lax.all_gather(value, "seq", axis=0, axis_index_groups=groups)
        return [every[b] for b in range(across)]

    def pick(stacked, index, axis=0):
        return lax.dynamic_index_in_dim(stacked, index, axis, keepdims=False)

    spots_x = [x, 1 - x] if across == 2 else list(range(across))

    def place(pieces, order, tie):
        pieces, _ = lax.optimization_barrier((pieces, tie))
        shape = (len(pieces), across) + pieces[0][0].shape
        placed = jnp.zeros(shape, pieces[0][0].dtype)
        for every, at in zip(pieces, order, strict=True):
            for piece, spot in zip(every, spots_x, strict=True):
                placed = lax.dynamic_update_slice(placed, piece[None, None], (at, spot, 0, 0))
        return placed.reshape(shape[0], shape[1] * shape[2], shape[3])

    def integers(values):
        return jnp.stack([jnp.asarray(v, jnp.int32) for v in values])

    def flat(lists):
        return [piece for every in lists for piece in every]

    def send_heads(by_head):
        return [pick(by_head, z)] + [swap_z(pick(by_head, z ^ k), k) for k in range(1, depth)]

    natural = [z ^ k for k in range(depth)]

    offsets = jnp.arange(windows_here, dtype=jnp.int32)[:, None] * window_cells
    picked = patches[(keep_lists + offsets).reshape(-1)]
    notes = jnp.concatenate([keep_lists.reshape(-1), visible_counts]).astype(jnp.bfloat16)
    notes = jnp.pad(notes[None], ((0, 15), (0, patch_in - notes.shape[0])))
    message = jnp.concatenate(
        [lax.dynamic_slice_in_dim(picked, t * quarter, quarter, 0), notes], axis=0
    )
    came = [swap_z(message, k) for k in range(1, depth)]
    remote = jnp.stack(came)
    remote_y = swap_t(remote, 2)
    both = jnp.stack([remote, remote_y])
    both_c = swap_t(both, 1)
    by_t = jnp.stack([both[0], both_c[0], both[1], both_c[1]])
    far = jnp.stack([pick(by_t, t ^ k)[:, :quarter] for k in range(tensor_count)], axis=1)
    tiles = jnp.concatenate([picked, far.reshape((depth - 1) * rows_here, patch_in)], axis=0)
    facts = jnp.concatenate([notes[:1], after(remote, remote_y)[:, quarter]]).astype(jnp.float32)
    keep = facts[:, :rows_here].astype(jnp.int32)
    counts = facts[:, rows_here : rows_here + windows_here].astype(jnp.int32)
    windows_held = depth * windows_here
    slot_ids = jnp.arange(slots, dtype=jnp.int32)
    visible = slot_ids[None, :] < counts.reshape(windows_held, 1)
    codes = jnp.where(visible, keep.reshape(windows_held, slots), -1)

    sent = send_heads(jnp.transpose(local_projection, (1, 0, 2)))
    sent_x = [from_x(sent[k]) for k in range(depth)]
    head_x = sent_x
    back_z = swap_z(local_output, 1)
    back_x = [from_x(local_output)]
    sent = send_heads(jnp.transpose(after(global_projection, remote_y), (1, 0, 2)))
    far_x = [from_x(sent[k]) for k in range(depth)]
    table_z = [global_output] + [swap_z(global_output, k) for k in range(1, depth)]
    table_x = [from_x(table_z[k]) for k in range(depth)]

    cell_ids = jnp.arange(window_cells, dtype=jnp.int32)
    hot = (keep.reshape(-1)[:, None] == cell_ids[None, :]).astype(jnp.bfloat16)
    embedded = jnp.dot(
        jnp.concatenate([tiles, hot], axis=1),
        jnp.concatenate([embed_weight, position_table], axis=0),
        preferred_element_type=jnp.float32,
    )
    start = embedded.astype(jnp.bfloat16)
    back_x.append(from_x(after(back_z, start)))
    local_full = place(head_x, natural, start).reshape(width, 3 * head)
    allowed = visible[:, None, :] | jnp.eye(slots, dtype=bool)[None]
    local_heads = jnp.dot(
        normed(start, local_gain), local_full, preferred_element_type=jnp.float32
    ).astype(jnp.bfloat16)
    local_mixed = local_attend(
        local_heads.reshape(windows_held, slots, 3 * head), allowed, head
    ).reshape(depth, rows_here, head)

    low, high, upper = t & 1, t >> 1, z >> 1
    bits = integers([upper, high, low, *natural])
    spots_whole = integers([*natural, *spots_x])
    spots_half = integers([z & 1, 1 - (z & 1), *spots_x])

    def gather_sum(keep, send):
        come = swap_t(send, 1)

        def part(index):
            return pick(keep, index) + pick(come, index).astype(jnp.float32)

        other = swap_t(part(1 - high).astype(jnp.bfloat16), 2)
        return part(high) + other.astype(jnp.float32)

    got = [jnp.stack([local_mixed[k], local_mixed[k ^ 2]]) for k in range(depth)]
    got = [got[0]] + [swap_z(got[k], k) for k in range(1, depth)]
    parts = project_back(bits, spots_half, got, flat(back_x), 2, share)
    start_here = lax.dynamic_slice(
        start, (2 * high * rows_here, (2 * upper + low) * share), (rows_here, share)
    )
    after_local = (start_here.astype(jnp.float32) + gather_sum(*parts)).astype(jnp.bfloat16)

    pieces = [after_local] + [swap_z(after_local, k) for k in (1, 2)]
    pieces.append(swap_z(after(after_local, pieces[1]), 3))
    pieces_y = [swap_t(pieces[k], 2) for k in range(depth)]
    far = [swap_t(pieces[k], 1) for k in range(depth)]
    far_y = [swap_t(pieces_y[k], 1) for k in range(depth)]
    gains = global_gain.reshape(tensor_count, 1, share)

    def project_planes(planes):
        groups = [[group[k] for k in planes] for group in (pieces, pieces_y, far, far_y)]
        return project_rows(bits, spots_whole, gains, *groups, flat(far_x), head)

    query_a, pairs_a = project_planes((0, 2))
    query_b, pairs_b = project_planes((1, 3))
    pairs_a, pairs_b = from_x(pairs_a), from_x(pairs_b)
    pairs = flat(zip(pairs_a, pairs_b, strict=True))
    turn = (0, 2, 1, 3)
    spot = 0 if across == 2 else x
    place_here = jnp.stack([keep[k] for k in turn]).reshape(all_rows, 1)
    codes_by_z = codes.reshape(depth, rows_here)
    every_code = from_x(jnp.stack([codes_by_z[k] for k in turn]).reshape(1, all_rows))
    own = jnp.full((1,), spot * all_rows, jnp.int32)
    tile = 512 // across
    if across == 2:
        so_far = global_attend(own, place_here, every_code[0], query_a, query_b, pairs[:2], tile)
        global_mixed = global_attend(
            tuple(so_far), place_here, every_code[1], query_a, query_b, pairs[2:], tile
        )
    else:
        codes_all = jnp.concatenate(every_code, axis=1)
        _, total, mixed = global_attend(own, place_here, codes_all, query_a, query_b, pairs, tile)
        global_mixed = (mixed / total).astype(query_a.dtype)
    global_mixed = global_mixed.reshape(depth, 1, rows_here, head)
    global_mixed = [global_mixed[k] for k in turn]
    got = [global_mixed[0]] + [swap_z(global_mixed[k], k) for k in range(1, depth)]
    parts = project_back(bits, spots_whole, got, flat(table_x), tensor_count, share)
    residual = jnp.where(
        upper == 0,
        jnp.where(high == 0, pieces[0], pieces[2]),
        jnp.where(high == 0, pieces_y[2], pieces_y[0]),
    )
    encoded = (residual.astype(jnp.float32) + gather_sum(*parts)).astype(jnp.bfloat16)
    own_codes = codes[:windows_here]
    cells_each = window_cells // seq_count
    cells = cell_ids.reshape(seq_count, 1, cells_each, 1)
    spread_hot = (own_codes[None, :, None, :] == cells).astype(jnp.bfloat16)
    spread = jnp.einsum(
        "swpj,wjd->swpd",
        spread_hot,
        encoded.reshape(windows_here, slots, share),
        preferred_element_type=jnp.float32,
    ).astype(jnp.bfloat16)
    result = lax.all_to_all(spread, "seq", split_axis=0, concat_axis=0, tiled=True)
    return result.reshape(seq_count * windows_here, cells_each, share)


def solution(mesh):
    run = place_and_run(mesh)
    return run


def place_and_run(mesh):
    placed = (
        P("seq", None),
        P("seq", None),
        P("seq"),
        P(),
        P(),
        P(),
        P("seq", "tensor", None),
        P("seq", "tensor"),
        P(),
        P("seq", "tensor", None),
        P("seq", "tensor"),
    )

    return jax.shard_map(
        shards, mesh=mesh, in_specs=placed, out_specs=P(None, "seq", "tensor"), check_vma=False
    )
```

```python
import functools
import math

import jax
import jax.numpy as jnp
from jax import lax
from jax.experimental import pallas as pl
from jax.experimental.pallas import tpu as pltpu
from jax.sharding import PartitionSpec as P


EPSILON = 1e-05


def normed(values, gain):
    floats = values.astype(jnp.float32)
    center = floats - jnp.mean(floats, axis=-1, keepdims=True)
    spread = jnp.mean(center * center, axis=-1, keepdims=True)
    return (center * lax.rsqrt(spread + EPSILON) * gain).astype(jnp.bfloat16)


def local_attend(heads, allowed, width):
    queries, key_part, value_part = (
        heads[..., :width],
        heads[..., width : 2 * width],
        heads[..., 2 * width :],
    )
    scores = jnp.einsum(
        "gqe,gke->gqk", queries, key_part, preferred_element_type=jnp.float32
    ) * width ** (-0.5)
    scores = jnp.where(allowed, scores, -jnp.inf)
    top = jnp.max(scores, axis=-1, keepdims=True)
    weights = jnp.exp(scores - top)
    weights = (weights / jnp.sum(weights, axis=-1, keepdims=True)).astype(jnp.bfloat16)
    return jnp.einsum("gqk,gke->gqe", weights, value_part, preferred_element_type=jnp.float32).astype(
        jnp.bfloat16
    )


def scores_over(query, place, ident, codes_ref, pair_refs, own):
    width = query.shape[1]
    factor = width ** (-0.5) * math.log2(math.e)
    parts, begin = [], 0
    for ref in pair_refs:
        keys = ref.shape[0]
        scores = lax.dot_general(
            query, ref[:, :width], (((1,), (1,)), ((), ())), preferred_element_type=jnp.float32
        )
        allowed = place == codes_ref[:, begin : begin + keys]
        if own:
            columns = lax.broadcasted_iota(jnp.int32, scores.shape, 1) + begin
            allowed = allowed | (ident == columns)
        parts.append(jnp.where(allowed, scores, -jnp.inf))
        begin += keys
    top = functools.reduce(jnp.maximum, [jnp.max(p, axis=-1, keepdims=True) for p in parts])
    return parts, top, factor


def weigh(parts, top, factor, pair_refs, width):
    total, mixed = 0.0, 0.0
    for ref, scores in zip(pair_refs, parts, strict=True):
        weights = jnp.exp2((scores - top) * factor)
        total = total + jnp.sum(weights, axis=-1, keepdims=True)
        mixed = mixed + jnp.dot(
            weights.astype(jnp.bfloat16), ref[:, width:], preferred_element_type=jnp.float32
        )
    return total, mixed


def own_kernel(own_ref, query_a, query_b, place_ref, codes_ref, *refs):
    *pair_refs, top_ref, total_ref, mixed_ref = refs
    tile, width = mixed_ref.shape
    step, half = pl.program_id(0), pl.num_programs(0) // 2
    query = jnp.where(step < half, query_a[...], query_b[...])
    ident = own_ref[0] + step * tile + lax.broadcasted_iota(jnp.int32, (tile, 1), 0)
    parts, top, factor = scores_over(query, place_ref[...], ident, codes_ref, pair_refs, True)
    total, mixed = weigh(parts, top, factor, pair_refs, width)
    top_ref[...], total_ref[...], mixed_ref[...] = top, total, mixed


def rest_kernel(query_a, query_b, place_ref, codes_ref, top_ref, total_ref, mixed_ref, *refs):
    *pair_refs, out0, out1, out2, out3 = refs
    width = out0.shape[2]
    step, half = pl.program_id(0), pl.num_programs(0) // 2
    query = jnp.where(step < half, query_a[...], query_b[...])
    parts, top, factor = scores_over(query, place_ref[...], None, codes_ref, pair_refs, False)
    before = top_ref[...]
    top = jnp.maximum(top, before)
    total, mixed = weigh(parts, top, factor, pair_refs, width)
    scale = jnp.exp2((before - top) * factor)
    total = total + total_ref[...] * scale
    result = ((mixed + mixed_ref[...] * scale) / total).astype(out0.dtype)
    for i, ref in enumerate((out0, out1, out2, out3)):

        @pl.when(step == i)
        def _(ref=ref):
            ref[0] = result


def global_attend(own, place, codes, query_a, query_b, pairs, tile):
    rows, width = query_a.shape
    half = rows // tile
    first = not isinstance(own, tuple)

    def by_tile(columns):
        return pl.BlockSpec((tile, columns), lambda i: (i, 0))

    specs = [
        pl.BlockSpec((tile, width), lambda i: (jnp.minimum(i, half - 1), 0)),
        pl.BlockSpec((tile, width), lambda i: (jnp.maximum(i - half, 0), 0)),
        by_tile(1),
        pl.BlockSpec(codes.shape, lambda i: (0, 0)),
    ]
    pair_specs = [pl.BlockSpec(p.shape, lambda i: (0, 0)) for p in pairs]
    kinds = [jax.ShapeDtypeStruct((2 * rows, c), jnp.float32) for c in (1, 1, width)]
    if first:
        return pl.pallas_call(
            own_kernel,
            grid=(2 * half,),
            in_specs=[pl.BlockSpec(memory_space=pltpu.SMEM), *specs, *pair_specs],
            out_specs=[by_tile(1), by_tile(1), by_tile(width)],
            out_shape=kinds,
            name="own_attend",
        )(own, query_a, query_b, place, codes, *pairs)
    return pl.pallas_call(
        rest_kernel,
        grid=(2 * half,),
        in_specs=[*specs, by_tile(1), by_tile(1), by_tile(width), *pair_specs],
        out_specs=[pl.BlockSpec((1, tile, width), lambda i: (0, 0, 0))] * 4,
        out_shape=[jax.ShapeDtypeStruct((1, tile, width), query_a.dtype)] * 4,
        name="rest_attend",
    )(query_a, query_b, place, codes, *own, *pairs)


def fill(table_ref, piece_refs, spots_ref):
    parts = table_ref.shape[0]
    across = len(piece_refs) // parts
    for i, ref in enumerate(piece_refs):
        at, spot = spots_ref[i // across], spots_ref[parts + i % across]
        rows = ref.shape[0]
        table_ref[at, pl.ds(pl.multiple_of(spot * rows, rows), rows), :] = ref[...]


def whole_vmem(count):
    return [pl.BlockSpec(memory_space=pltpu.VMEM)] * count


def rows_kernel(bits_ref, spots_ref, gains_ref, *refs):
    *refs, query_ref, pair_ref, table_ref = refs
    own, own_y, far, far_y = refs[0:2], refs[2:4], refs[4:6], refs[6:8]
    fill(table_ref, refs[8:], spots_ref)
    upper, high, low = bits_ref[0], bits_ref[1], bits_ref[2]
    rows, width = own[0].shape[0], query_ref.shape[1]
    choices = (
        (high, (own[0], far[0], own_y[1], far_y[1])),
        (1 - high, (own_y[0], far_y[0], own[1], far[1])),
    )
    for row, parts in choices:
        floats = [ref[...].astype(jnp.float32) for ref in parts]
        count = sum(f.shape[1] for f in floats)
        mean = sum(jnp.sum(f, axis=-1, keepdims=True) for f in floats) / count
        floats = [f - mean for f in floats]
        spread = sum(jnp.sum(f * f, axis=-1, keepdims=True) for f in floats) / count
        total = None
        for i, f in enumerate(floats):
            half = upper if i < 2 else 1 - upper
            quarter = 2 * half + (low if i % 2 == 0 else 1 - low)
            ready = (f * gains_ref[quarter]).astype(jnp.bfloat16)
            product = jnp.dot(ready, table_ref[quarter], preferred_element_type=jnp.float32)
            total = product if total is None else total + product
        heads = (total * lax.rsqrt(spread + EPSILON)).astype(query_ref.dtype)
        begin = pl.multiple_of(row * rows, rows)
        query_ref[pl.ds(begin, rows), :] = heads[:, :width]
        pair_ref[pl.ds(begin, rows), :] = heads[:, width:]


def project_rows(bits, spots, gains, own, own_y, far, far_y, pieces, head):
    rows, share = own[0].shape
    operands = [*own, *own_y, *far, *far_y, *pieces]
    kind = own[0].dtype
    return pl.pallas_call(
        rows_kernel,
        in_specs=[pl.BlockSpec(memory_space=pltpu.SMEM)] * 2 + whole_vmem(1 + len(operands)),
        out_specs=whole_vmem(2),
        out_shape=[
            jax.ShapeDtypeStruct((2 * rows, head), kind),
            jax.ShapeDtypeStruct((2 * rows, 2 * head), kind),
        ],
        scratch_shapes=[pltpu.VMEM((gains.shape[0], share, 3 * head), kind)],
        name="project_rows",
    )(bits, spots, gains, *operands)


def back_kernel(bits_ref, spots_ref, *refs):
    *refs, keep_ref, send_ref, row_ref, table_ref = refs
    depth = row_ref.shape[2] // refs[0].shape[2]
    fill(table_ref, refs[depth:], spots_ref)
    low, head = bits_ref[2], refs[0].shape[2]
    for k in range(depth):
        begin = pl.multiple_of(bits_ref[3 + k] * head, head)
        row_ref[:, :, pl.ds(begin, head)] = refs[k][...]
    contract = (((1,), (1,)), ((), ()))
    apart = row_ref.shape[0] == 2
    for i in range(2):
        row = row_ref[i if apart else 0]
        keep, send = (low, 1 - low) if apart else (2 * i + low, 2 * i + 1 - low)
        keep_ref[i] = lax.dot_general(
            row, table_ref[keep], contract, preferred_element_type=jnp.float32
        )
        send_ref[i] = lax.dot_general(
            row, table_ref[send], contract, preferred_element_type=jnp.float32
        ).astype(send_ref.dtype)


def project_back(bits, spots, mixed, pieces, parts, share):
    groups, rows, head = mixed[0].shape
    kind = mixed[0].dtype
    width = len(mixed) * head
    return pl.pallas_call(
        back_kernel,
        in_specs=[pl.BlockSpec(memory_space=pltpu.SMEM)] * 2
        + whole_vmem(len(mixed) + len(pieces)),
        out_specs=whole_vmem(2),
        out_shape=[
            jax.ShapeDtypeStruct((2, rows, share), jnp.float32),
            jax.ShapeDtypeStruct((2, rows, share), kind),
        ],
        scratch_shapes=[
            pltpu.VMEM((groups, rows, width), kind),
            pltpu.VMEM((parts, share, width), kind),
        ],
        name="project_back",
    )(bits, spots, *mixed, *pieces)


def after(value, *others):
    return lax.optimization_barrier((value, *others))[0]


def shards(
    patches,
    keep_lists,
    visible_counts,
    embed_weight,
    position_table,
    local_gain,
    local_projection,
    local_output,
    global_gain,
    global_projection,
    global_output,
):
    windows_here, slots = keep_lists.shape
    window_cells, width = position_table.shape
    heads_here = local_projection.shape[1]
    head = local_projection.shape[2] // 3
    seq_count = lax.axis_size("seq")
    tensor_count = lax.axis_size("tensor")
    share = width // tensor_count
    depth = heads_here
    across = seq_count // depth
    assert depth == 4 and tensor_count == 4 and across * depth == seq_count
    rows_here = windows_here * slots
    all_rows = depth * rows_here
    patch_in = patches.shape[1]
    quarter = rows_here // tensor_count
    s = lax.axis_index("seq")
    t = lax.axis_index("tensor")
    z = s // across
    x = s % across

    def swap_z(value, k):
        return lax.ppermute(
            value,
            "seq",
            [(a * across + b, (a ^ k) * across + b) for a in range(depth) for b in range(across)],
        )

    def swap_t(value, k):
        return lax.ppermute(value, "tensor", [(a, a ^ k) for a in range(tensor_count)])

    def from_x(value):
        if across == 2:
            return [value, lax.ppermute(value, "seq", [(a, a ^ 1) for a in range(seq_count)])]
        groups = [[a * across + b for b in range(across)] for a in range(depth)]
        every = lax.all_gather(value, "seq", axis=0, axis_index_groups=groups)
        return [every[b] for b in range(across)]

    def pick(stacked, index, axis=0):
        return lax.dynamic_index_in_dim(stacked, index, axis, keepdims=False)

    spots_x = [x, 1 - x] if across == 2 else list(range(across))

    def place(pieces, order, tie):
        pieces, _ = lax.optimization_barrier((pieces, tie))
        shape = (len(pieces), across) + pieces[0][0].shape
        placed = jnp.zeros(shape, pieces[0][0].dtype)
        for every, at in zip(pieces, order, strict=True):
            for piece, spot in zip(every, spots_x, strict=True):
                placed = lax.dynamic_update_slice(placed, piece[None, None], (at, spot, 0, 0))
        return placed.reshape(shape[0], shape[1] * shape[2], shape[3])

    def integers(values):
        return jnp.stack([jnp.asarray(v, jnp.int32) for v in values])

    def flat(lists):
        return [piece for every in lists for piece in every]

    def send_heads(by_head):
        return [pick(by_head, z)] + [swap_z(pick(by_head, z ^ k), k) for k in range(1, depth)]

    natural = [z ^ k for k in range(depth)]

    offsets = jnp.arange(windows_here, dtype=jnp.int32)[:, None] * window_cells
    picked = patches[(keep_lists + offsets).reshape(-1)]
    notes = jnp.concatenate([keep_lists.reshape(-1), visible_counts]).astype(jnp.bfloat16)
    notes = jnp.pad(notes[None], ((0, 15), (0, patch_in - notes.shape[0])))
    message = jnp.concatenate(
        [lax.dynamic_slice_in_dim(picked, t * quarter, quarter, 0), notes], axis=0
    )
    came = [swap_z(message, k) for k in range(1, depth)]
    remote = jnp.stack(came)
    remote_y = swap_t(remote, 2)
    both = jnp.stack([remote, remote_y])
    both_c = swap_t(both, 1)
    by_t = jnp.stack([both[0], both_c[0], both[1], both_c[1]])
    far = jnp.stack([pick(by_t, t ^ k)[:, :quarter] for k in range(tensor_count)], axis=1)
    tiles = jnp.concatenate([picked, far.reshape((depth - 1) * rows_here, patch_in)], axis=0)
    facts = jnp.concatenate([notes[:1], after(remote, remote_y)[:, quarter]]).astype(jnp.float32)
    keep = facts[:, :rows_here].astype(jnp.int32)
    counts = facts[:, rows_here : rows_here + windows_here].astype(jnp.int32)
    windows_held = depth * windows_here
    slot_ids = jnp.arange(slots, dtype=jnp.int32)
    visible = slot_ids[None, :] < counts.reshape(windows_held, 1)
    codes = jnp.where(visible, keep.reshape(windows_held, slots), -1)

    sent = send_heads(jnp.transpose(local_projection, (1, 0, 2)))
    sent_x = [from_x(sent[k]) for k in range(depth)]
    head_x = sent_x
    back_z = swap_z(local_output, 1)
    back_x = [from_x(local_output)]
    sent = send_heads(jnp.transpose(after(global_projection, remote_y), (1, 0, 2)))
    far_x = [from_x(sent[k]) for k in range(depth)]
    table_z = [global_output] + [swap_z(global_output, k) for k in range(1, depth)]
    table_x = [from_x(table_z[k]) for k in range(depth)]

    cell_ids = jnp.arange(window_cells, dtype=jnp.int32)
    hot = (keep.reshape(-1)[:, None] == cell_ids[None, :]).astype(jnp.bfloat16)
    embedded = jnp.dot(
        jnp.concatenate([tiles, hot], axis=1),
        jnp.concatenate([embed_weight, position_table], axis=0),
        preferred_element_type=jnp.float32,
    )
    start = embedded.astype(jnp.bfloat16)
    back_x.append(from_x(after(back_z, start)))
    local_full = place(head_x, natural, start).reshape(width, 3 * head)
    allowed = visible[:, None, :] | jnp.eye(slots, dtype=bool)[None]
    local_heads = jnp.dot(
        normed(start, local_gain), local_full, preferred_element_type=jnp.float32
    ).astype(jnp.bfloat16)
    local_mixed = local_attend(
        local_heads.reshape(windows_held, slots, 3 * head), allowed, head
    ).reshape(depth, rows_here, head)

    low, high, upper = t & 1, t >> 1, z >> 1
    bits = integers([upper, high, low, *natural])
    spots_whole = integers([*natural, *spots_x])
    spots_half = integers([z & 1, 1 - (z & 1), *spots_x])

    def gather_sum(keep, send):
        come = swap_t(send, 1)

        def part(index):
            return pick(keep, index) + pick(come, index).astype(jnp.float32)

        other = swap_t(part(1 - high).astype(jnp.bfloat16), 2)
        return part(high) + other.astype(jnp.float32)

    got = [jnp.stack([local_mixed[k], local_mixed[k ^ 2]]) for k in range(depth)]
    got = [got[0]] + [swap_z(got[k], k) for k in range(1, depth)]
    parts = project_back(bits, spots_half, got, flat(back_x), 2, share)
    start_here = lax.dynamic_slice(
        start, (2 * high * rows_here, (2 * upper + low) * share), (rows_here, share)
    )
    after_local = (start_here.astype(jnp.float32) + gather_sum(*parts)).astype(jnp.bfloat16)

    pieces = [after_local] + [swap_z(after_local, k) for k in (1, 2)]
    pieces.append(swap_z(after(after_local, pieces[1]), 3))
    pieces_y = [swap_t(pieces[k], 2) for k in range(depth)]
    far = [swap_t(pieces[k], 1) for k in range(depth)]
    far_y = [swap_t(pieces_y[k], 1) for k in range(depth)]
    gains = global_gain.reshape(tensor_count, 1, share)

    def project_planes(planes):
        groups = [[group[k] for k in planes] for group in (pieces, pieces_y, far, far_y)]
        return project_rows(bits, spots_whole, gains, *groups, flat(far_x), head)

    query_a, pairs_a = project_planes((0, 2))
    query_b, pairs_b = project_planes((1, 3))
    pairs_a, pairs_b = from_x(pairs_a), from_x(pairs_b)
    pairs = flat(zip(pairs_a, pairs_b, strict=True))
    turn = (0, 2, 1, 3)
    spot = 0 if across == 2 else x
    place_here = jnp.stack([keep[k] for k in turn]).reshape(all_rows, 1)
    codes_by_z = codes.reshape(depth, rows_here)
    every_code = from_x(jnp.stack([codes_by_z[k] for k in turn]).reshape(1, all_rows))
    own = jnp.full((1,), spot * all_rows, jnp.int32)
    tile = 512 // across
    if across == 2:
        so_far = global_attend(own, place_here, every_code[0], query_a, query_b, pairs[:2], tile)
        global_mixed = global_attend(
            tuple(so_far), place_here, every_code[1], query_a, query_b, pairs[2:], tile
        )
    else:
        codes_all = jnp.concatenate(every_code, axis=1)
        _, total, mixed = global_attend(own, place_here, codes_all, query_a, query_b, pairs, tile)
        global_mixed = (mixed / total).astype(query_a.dtype).reshape(depth, 1, rows_here, head)
    global_mixed = [global_mixed[k] for k in turn]
    got = [global_mixed[0]] + [swap_z(global_mixed[k], k) for k in range(1, depth)]
    parts = project_back(bits, spots_whole, got, flat(table_x), tensor_count, share)
    residual = jnp.where(
        upper == 0,
        jnp.where(high == 0, pieces[0], pieces[2]),
        jnp.where(high == 0, pieces_y[2], pieces_y[0]),
    )
    encoded = (residual.astype(jnp.float32) + gather_sum(*parts)).astype(jnp.bfloat16)
    own_codes = codes[:windows_here]
    cells_each = window_cells // seq_count
    cells = cell_ids.reshape(seq_count, 1, cells_each, 1)
    spread_hot = (own_codes[None, :, None, :] == cells).astype(jnp.bfloat16)
    spread = jnp.einsum(
        "swpj,wjd->swpd",
        spread_hot,
        encoded.reshape(windows_here, slots, share),
        preferred_element_type=jnp.float32,
    ).astype(jnp.bfloat16)
    result = lax.all_to_all(spread, "seq", split_axis=0, concat_axis=0, tiled=True)
    return result.reshape(seq_count * windows_here, cells_each, share)


def solution(mesh):
    run = place_and_run(mesh)
    return run


def place_and_run(mesh):
    placed = (
        P("seq", None),
        P("seq", None),
        P("seq"),
        P(),
        P(),
        P(),
        P("seq", "tensor", None),
        P("seq", "tensor"),
        P(),
        P("seq", "tensor", None),
        P("seq", "tensor"),
    )

    return jax.shard_map(
        shards, mesh=mesh, in_specs=placed, out_specs=P(None, "seq", "tensor"), check_vma=False
    )
```

```python
import functools
import math

import jax
import jax.numpy as jnp
from jax import lax
from jax.experimental import pallas as pl
from jax.experimental.pallas import tpu as pltpu
from jax.sharding import PartitionSpec as P


EPSILON = 1e-05


def normed(values, gain):
    floats = values.astype(jnp.float32)
    center = floats - jnp.mean(floats, axis=-1, keepdims=True)
    spread = jnp.mean(center * center, axis=-1, keepdims=True)
    return (center * lax.rsqrt(spread + EPSILON) * gain).astype(jnp.bfloat16)


def local_attend(heads, allowed, width):
    queries, key_part, value_part = (
        heads[..., :width],
        heads[..., width : 2 * width],
        heads[..., 2 * width :],
    )
    scores = jnp.einsum(
        "gqe,gke->gqk", queries, key_part, preferred_element_type=jnp.float32
    ) * width ** (-0.5)
    scores = jnp.where(allowed, scores, -jnp.inf)
    top = jnp.max(scores, axis=-1, keepdims=True)
    weights = jnp.exp(scores - top)
    weights = (weights / jnp.sum(weights, axis=-1, keepdims=True)).astype(jnp.bfloat16)
    return jnp.einsum("gqk,gke->gqe", weights, value_part, preferred_element_type=jnp.float32).astype(
        jnp.bfloat16
    )


def scores_over(query, place, ident, codes_ref, pair_refs, own):
    width = query.shape[1]
    factor = width ** (-0.5) * math.log2(math.e)
    parts, begin = [], 0
    for ref in pair_refs:
        keys = ref.shape[0]
        scores = lax.dot_general(
            query, ref[:, :width], (((1,), (1,)), ((), ())), preferred_element_type=jnp.float32
        )
        allowed = place == codes_ref[:, begin : begin + keys]
        if own:
            columns = lax.broadcasted_iota(jnp.int32, scores.shape, 1) + begin
            allowed = allowed | (ident == columns)
        parts.append(jnp.where(allowed, scores, -jnp.inf))
        begin += keys
    top = functools.reduce(jnp.maximum, [jnp.max(p, axis=-1, keepdims=True) for p in parts])
    return parts, top, factor


def weigh(parts, top, factor, pair_refs, width):
    total, mixed = 0.0, 0.0
    for ref, scores in zip(pair_refs, parts, strict=True):
        weights = jnp.exp2((scores - top) * factor)
        total = total + jnp.sum(weights, axis=-1, keepdims=True)
        mixed = mixed + jnp.dot(
            weights.astype(jnp.bfloat16), ref[:, width:], preferred_element_type=jnp.float32
        )
    return total, mixed


def own_kernel(own_ref, query_a, query_b, place_ref, codes_ref, *refs):
    *pair_refs, top_ref, total_ref, mixed_ref = refs
    tile, width = mixed_ref.shape
    step, half = pl.program_id(0), pl.num_programs(0) // 2
    query = jnp.where(step < half, query_a[...], query_b[...])
    ident = own_ref[0] + step * tile + lax.broadcasted_iota(jnp.int32, (tile, 1), 0)
    parts, top, factor = scores_over(query, place_ref[...], ident, codes_ref, pair_refs, True)
    total, mixed = weigh(parts, top, factor, pair_refs, width)
    top_ref[...], total_ref[...], mixed_ref[...] = top, total, mixed


def rest_kernel(query_a, query_b, place_ref, codes_ref, top_ref, total_ref, mixed_ref, *refs):
    *pair_refs, out0, out1, out2, out3 = refs
    width = out0.shape[2]
    step, half = pl.program_id(0), pl.num_programs(0) // 2
    query = jnp.where(step < half, query_a[...], query_b[...])
    parts, top, factor = scores_over(query, place_ref[...], None, codes_ref, pair_refs, False)
    before = top_ref[...]
    top = jnp.maximum(top, before)
    total, mixed = weigh(parts, top, factor, pair_refs, width)
    scale = jnp.exp2((before - top) * factor)
    total = total + total_ref[...] * scale
    result = ((mixed + mixed_ref[...] * scale) / total).astype(out0.dtype)
    for i, ref in enumerate((out0, out1, out2, out3)):

        @pl.when(step == i)
        def _(ref=ref):
            ref[0] = result


def global_attend(own, place, codes, query_a, query_b, pairs, tile):
    rows, width = query_a.shape
    half = rows // tile
    first = not isinstance(own, tuple)

    def by_tile(columns):
        return pl.BlockSpec((tile, columns), lambda i: (i, 0))

    specs = [
        pl.BlockSpec((tile, width), lambda i: (jnp.minimum(i, half - 1), 0)),
        pl.BlockSpec((tile, width), lambda i: (jnp.maximum(i - half, 0), 0)),
        by_tile(1),
        pl.BlockSpec(codes.shape, lambda i: (0, 0)),
    ]
    pair_specs = [pl.BlockSpec(p.shape, lambda i: (0, 0)) for p in pairs]
    kinds = [jax.ShapeDtypeStruct((2 * rows, c), jnp.float32) for c in (1, 1, width)]
    if first:
        return pl.pallas_call(
            own_kernel,
            grid=(2 * half,),
            in_specs=[pl.BlockSpec(memory_space=pltpu.SMEM), *specs, *pair_specs],
            out_specs=[by_tile(1), by_tile(1), by_tile(width)],
            out_shape=kinds,
            name="own_attend",
        )(own, query_a, query_b, place, codes, *pairs)
    return pl.pallas_call(
        rest_kernel,
        grid=(2 * half,),
        in_specs=[*specs, by_tile(1), by_tile(1), by_tile(width), *pair_specs],
        out_specs=[pl.BlockSpec((1, tile, width), lambda i: (0, 0, 0))] * 4,
        out_shape=[jax.ShapeDtypeStruct((1, tile, width), query_a.dtype)] * 4,
        name="rest_attend",
    )(query_a, query_b, place, codes, *own, *pairs)


def fill(table_ref, piece_refs, spots_ref):
    parts = table_ref.shape[0]
    across = len(piece_refs) // parts
    for i, ref in enumerate(piece_refs):
        at, spot = spots_ref[i // across], spots_ref[parts + i % across]
        rows = ref.shape[0]
        table_ref[at, pl.ds(pl.multiple_of(spot * rows, rows), rows), :] = ref[...]


def whole_vmem(count):
    return [pl.BlockSpec(memory_space=pltpu.VMEM)] * count


def rows_kernel(bits_ref, spots_ref, gains_ref, *refs):
    *refs, query_ref, pair_ref, table_ref = refs
    own, own_y, far, far_y = refs[0:2], refs[2:4], refs[4:6], refs[6:8]
    fill(table_ref, refs[8:], spots_ref)
    upper, high, low = bits_ref[0], bits_ref[1], bits_ref[2]
    rows, width = own[0].shape[0], query_ref.shape[1]
    choices = (
        (high, (own[0], far[0], own_y[1], far_y[1])),
        (1 - high, (own_y[0], far_y[0], own[1], far[1])),
    )
    for row, parts in choices:
        floats = [ref[...].astype(jnp.float32) for ref in parts]
        count = sum(f.shape[1] for f in floats)
        mean = sum(jnp.sum(f, axis=-1, keepdims=True) for f in floats) / count
        floats = [f - mean for f in floats]
        spread = sum(jnp.sum(f * f, axis=-1, keepdims=True) for f in floats) / count
        total = None
        for i, f in enumerate(floats):
            half = upper if i < 2 else 1 - upper
            quarter = 2 * half + (low if i % 2 == 0 else 1 - low)
            ready = (f * gains_ref[quarter]).astype(jnp.bfloat16)
            product = jnp.dot(ready, table_ref[quarter], preferred_element_type=jnp.float32)
            total = product if total is None else total + product
        heads = (total * lax.rsqrt(spread + EPSILON)).astype(query_ref.dtype)
        begin = pl.multiple_of(row * rows, rows)
        query_ref[pl.ds(begin, rows), :] = heads[:, :width]
        pair_ref[pl.ds(begin, rows), :] = heads[:, width:]


def project_rows(bits, spots, gains, own, own_y, far, far_y, pieces, head):
    rows, share = own[0].shape
    operands = [*own, *own_y, *far, *far_y, *pieces]
    kind = own[0].dtype
    return pl.pallas_call(
        rows_kernel,
        in_specs=[pl.BlockSpec(memory_space=pltpu.SMEM)] * 2 + whole_vmem(1 + len(operands)),
        out_specs=whole_vmem(2),
        out_shape=[
            jax.ShapeDtypeStruct((2 * rows, head), kind),
            jax.ShapeDtypeStruct((2 * rows, 2 * head), kind),
        ],
        scratch_shapes=[pltpu.VMEM((gains.shape[0], share, 3 * head), kind)],
        name="project_rows",
    )(bits, spots, gains, *operands)


def back_kernel(bits_ref, spots_ref, *refs):
    *refs, keep_ref, send_ref, row_ref, table_ref = refs
    depth = row_ref.shape[2] // refs[0].shape[2]
    fill(table_ref, refs[depth:], spots_ref)
    low, head = bits_ref[2], refs[0].shape[2]
    for k in range(depth):
        begin = pl.multiple_of(bits_ref[3 + k] * head, head)
        row_ref[:, :, pl.ds(begin, head)] = refs[k][...]
    contract = (((1,), (1,)), ((), ()))
    apart = row_ref.shape[0] == 2
    for i in range(2):
        row = row_ref[i if apart else 0]
        keep, send = (low, 1 - low) if apart else (2 * i + low, 2 * i + 1 - low)
        keep_ref[i] = lax.dot_general(
            row, table_ref[keep], contract, preferred_element_type=jnp.float32
        )
        send_ref[i] = lax.dot_general(
            row, table_ref[send], contract, preferred_element_type=jnp.float32
        ).astype(send_ref.dtype)


def project_back(bits, spots, mixed, pieces, parts, share):
    groups, rows, head = mixed[0].shape
    kind = mixed[0].dtype
    width = len(mixed) * head
    return pl.pallas_call(
        back_kernel,
        in_specs=[pl.BlockSpec(memory_space=pltpu.SMEM)] * 2
        + whole_vmem(len(mixed) + len(pieces)),
        out_specs=whole_vmem(2),
        out_shape=[
            jax.ShapeDtypeStruct((2, rows, share), jnp.float32),
            jax.ShapeDtypeStruct((2, rows, share), kind),
        ],
        scratch_shapes=[
            pltpu.VMEM((groups, rows, width), kind),
            pltpu.VMEM((parts, share, width), kind),
        ],
        name="project_back",
    )(bits, spots, *mixed, *pieces)


def after(value, *others):
    return lax.optimization_barrier((value, *others))[0]


def shards(
    patches,
    keep_lists,
    visible_counts,
    embed_weight,
    position_table,
    local_gain,
    local_projection,
    local_output,
    global_gain,
    global_projection,
    global_output,
):
    windows_here, slots = keep_lists.shape
    window_cells, width = position_table.shape
    heads_here = local_projection.shape[1]
    head = local_projection.shape[2] // 3
    seq_count = lax.axis_size("seq")
    tensor_count = lax.axis_size("tensor")
    share = width // tensor_count
    depth = heads_here
    across = seq_count // depth
    assert depth == 4 and tensor_count == 4 and across * depth == seq_count
    rows_here = windows_here * slots
    all_rows = depth * rows_here
    patch_in = patches.shape[1]
    quarter = rows_here // tensor_count
    s = lax.axis_index("seq")
    t = lax.axis_index("tensor")
    z = s // across
    x = s % across

    def swap_z(value, k):
        return lax.ppermute(
            value,
            "seq",
            [(a * across + b, (a ^ k) * across + b) for a in range(depth) for b in range(across)],
        )

    def swap_t(value, k):
        return lax.ppermute(value, "tensor", [(a, a ^ k) for a in range(tensor_count)])

    def from_x(value):
        if across == 2:
            return [value, lax.ppermute(value, "seq", [(a, a ^ 1) for a in range(seq_count)])]
        groups = [[a * across + b for b in range(across)] for a in range(depth)]
        every = lax.all_gather(value, "seq", axis=0, axis_index_groups=groups)
        return [every[b] for b in range(across)]

    def pick(stacked, index, axis=0):
        return lax.dynamic_index_in_dim(stacked, index, axis, keepdims=False)

    spots_x = [x, 1 - x] if across == 2 else list(range(across))

    def place(pieces, order, tie):
        pieces, _ = lax.optimization_barrier((pieces, tie))
        shape = (len(pieces), across) + pieces[0][0].shape
        placed = jnp.zeros(shape, pieces[0][0].dtype)
        for every, at in zip(pieces, order, strict=True):
            if across == 2:
                first = x == 0
                every = [jnp.where(first, *every), jnp.where(first, every[1], every[0])]
            placed = lax.dynamic_update_slice(placed, jnp.stack(every)[None], (at, 0, 0, 0))
        return placed.reshape(shape[0], shape[1] * shape[2], shape[3])

    def integers(values):
        return jnp.stack([jnp.asarray(v, jnp.int32) for v in values])

    def flat(lists):
        return [piece for every in lists for piece in every]

    def send_heads(by_head):
        return [pick(by_head, z)] + [swap_z(pick(by_head, z ^ k), k) for k in range(1, depth)]

    natural = [z ^ k for k in range(depth)]

    offsets = jnp.arange(windows_here, dtype=jnp.int32)[:, None] * window_cells
    picked = patches[(keep_lists + offsets).reshape(-1)]
    notes = jnp.concatenate([keep_lists.reshape(-1), visible_counts]).astype(jnp.bfloat16)
    notes = jnp.pad(notes[None], ((0, 15), (0, patch_in - notes.shape[0])))
    message = jnp.concatenate(
        [lax.dynamic_slice_in_dim(picked, t * quarter, quarter, 0), notes], axis=0
    )
    came = [swap_z(message, k) for k in range(1, depth)]
    remote = jnp.stack(came)
    remote_y = swap_t(remote, 2)
    both = jnp.stack([remote, remote_y])
    both_c = swap_t(both, 1)
    by_t = jnp.stack([both[0], both_c[0], both[1], both_c[1]])
    far = jnp.stack([pick(by_t, t ^ k)[:, :quarter] for k in range(tensor_count)], axis=1)
    tiles = jnp.concatenate([picked, far.reshape((depth - 1) * rows_here, patch_in)], axis=0)
    facts = jnp.concatenate([notes[:1], after(remote, remote_y)[:, quarter]]).astype(jnp.float32)
    keep = facts[:, :rows_here].astype(jnp.int32)
    counts = facts[:, rows_here : rows_here + windows_here].astype(jnp.int32)
    windows_held = depth * windows_here
    slot_ids = jnp.arange(slots, dtype=jnp.int32)
    visible = slot_ids[None, :] < counts.reshape(windows_held, 1)
    codes = jnp.where(visible, keep.reshape(windows_held, slots), -1)

    sent = send_heads(jnp.transpose(local_projection, (1, 0, 2)))
    sent_x = [from_x(sent[k]) for k in range(depth)]
    head_x = sent_x
    back_z = swap_z(local_output, 1)
    back_x = [from_x(local_output)]
    sent = send_heads(jnp.transpose(after(global_projection, remote_y), (1, 0, 2)))
    far_x = [from_x(sent[k]) for k in range(depth)]
    table_z = [global_output] + [swap_z(global_output, k) for k in range(1, depth)]
    table_x = [from_x(table_z[k]) for k in range(depth)]

    cell_ids = jnp.arange(window_cells, dtype=jnp.int32)
    hot = (keep.reshape(-1)[:, None] == cell_ids[None, :]).astype(jnp.bfloat16)
    embedded = jnp.dot(
        jnp.concatenate([tiles, hot], axis=1),
        jnp.concatenate([embed_weight, position_table], axis=0),
        preferred_element_type=jnp.float32,
    )
    start = embedded.astype(jnp.bfloat16)
    back_x.append(from_x(after(back_z, start)))
    local_full = place(head_x, natural, start).reshape(width, 3 * head)
    allowed = visible[:, None, :] | jnp.eye(slots, dtype=bool)[None]
    local_heads = jnp.dot(
        normed(start, local_gain), local_full, preferred_element_type=jnp.float32
    ).astype(jnp.bfloat16)
    local_mixed = local_attend(
        local_heads.reshape(windows_held, slots, 3 * head), allowed, head
    ).reshape(depth, rows_here, head)

    low, high, upper = t & 1, t >> 1, z >> 1
    bits = integers([upper, high, low, *natural])
    spots_whole = integers([*natural, *spots_x])
    spots_half = integers([z & 1, 1 - (z & 1), *spots_x])

    def gather_sum(keep, send):
        come = swap_t(send, 1)

        def part(index):
            return pick(keep, index) + pick(come, index).astype(jnp.float32)

        other = swap_t(part(1 - high).astype(jnp.bfloat16), 2)
        return part(high) + other.astype(jnp.float32)

    got = [jnp.stack([local_mixed[k], local_mixed[k ^ 2]]) for k in range(depth)]
    got = [got[0]] + [swap_z(got[k], k) for k in range(1, depth)]
    parts = project_back(bits, spots_half, got, flat(back_x), 2, share)
    start_here = lax.dynamic_slice(
        start, (2 * high * rows_here, (2 * upper + low) * share), (rows_here, share)
    )
    after_local = (start_here.astype(jnp.float32) + gather_sum(*parts)).astype(jnp.bfloat16)

    pieces = [after_local] + [swap_z(after_local, k) for k in (1, 2)]
    pieces.append(swap_z(after(after_local, pieces[1]), 3))
    pieces_y = [swap_t(pieces[k], 2) for k in range(depth)]
    far = [swap_t(pieces[k], 1) for k in range(depth)]
    far_y = [swap_t(pieces_y[k], 1) for k in range(depth)]
    gains = global_gain.reshape(tensor_count, 1, share)

    def project_planes(planes):
        groups = [[group[k] for k in planes] for group in (pieces, pieces_y, far, far_y)]
        return project_rows(bits, spots_whole, gains, *groups, flat(far_x), head)

    query_a, pairs_a = project_planes((0, 2))
    query_b, pairs_b = project_planes((1, 3))
    pairs_a, pairs_b = from_x(pairs_a), from_x(pairs_b)
    pairs = flat(zip(pairs_a, pairs_b, strict=True))
    turn = (0, 2, 1, 3)
    spot = 0 if across == 2 else x
    place_here = jnp.stack([keep[k] for k in turn]).reshape(all_rows, 1)
    codes_by_z = codes.reshape(depth, rows_here)
    every_code = from_x(jnp.stack([codes_by_z[k] for k in turn]).reshape(1, all_rows))
    own = jnp.full((1,), spot * all_rows, jnp.int32)
    tile = 512 // across
    if across == 2:
        so_far = global_attend(own, place_here, every_code[0], query_a, query_b, pairs[:2], tile)
        global_mixed = global_attend(
            tuple(so_far), place_here, every_code[1], query_a, query_b, pairs[2:], tile
        )
    else:
        codes_all = jnp.concatenate(every_code, axis=1)
        _, total, mixed = global_attend(own, place_here, codes_all, query_a, query_b, pairs, tile)
        global_mixed = (mixed / total).astype(query_a.dtype).reshape(depth, 1, rows_here, head)
    global_mixed = [global_mixed[k] for k in turn]
    got = [global_mixed[0]] + [swap_z(global_mixed[k], k) for k in range(1, depth)]
    parts = project_back(bits, spots_whole, got, flat(table_x), tensor_count, share)
    residual = jnp.where(
        upper == 0,
        jnp.where(high == 0, pieces[0], pieces[2]),
        jnp.where(high == 0, pieces_y[2], pieces_y[0]),
    )
    encoded = (residual.astype(jnp.float32) + gather_sum(*parts)).astype(jnp.bfloat16)
    own_codes = codes[:windows_here]
    cells_each = window_cells // seq_count
    cells = cell_ids.reshape(seq_count, 1, cells_each, 1)
    spread_hot = (own_codes[None, :, None, :] == cells).astype(jnp.bfloat16)
    spread = jnp.einsum(
        "swpj,wjd->swpd",
        spread_hot,
        encoded.reshape(windows_here, slots, share),
        preferred_element_type=jnp.float32,
    ).astype(jnp.bfloat16)
    result = lax.all_to_all(spread, "seq", split_axis=0, concat_axis=0, tiled=True)
    return result.reshape(seq_count * windows_here, cells_each, share)


def solution(mesh):
    run = place_and_run(mesh)
    return run


def place_and_run(mesh):
    placed = (
        P("seq", None),
        P("seq", None),
        P("seq"),
        P(),
        P(),
        P(),
        P("seq", "tensor", None),
        P("seq", "tensor"),
        P(),
        P("seq", "tensor", None),
        P("seq", "tensor"),
    )

    return jax.shard_map(
        shards, mesh=mesh, in_specs=placed, out_specs=P(None, "seq", "tensor"), check_vma=False
    )
```
